32 devices in a mesh: seq: 2 (over y), shard: 4 (over x, core), rep: 4 (over z).
Axes of the slice: x: 2, y: 2, z: 4, core: 2. Of those that a mesh axis runs over, the one named last changes fastest.
Arguments:
- tokens: bfloat16 [16, 580, 1024], P(('shard', 'rep'), 'seq'), may hold values from -6 to 6
- lengths: int32 [16], P(('shard', 'rep')), may hold values from 435 to 580, as said below
- qkv_weight: bfloat16 [1024, 3072], P('shard'), may hold values from -0.1875 to 0.1875
- query_bias: bfloat16 [1024], P('shard'), may hold values from -3 to 3
- value_bias: bfloat16 [1024], P('shard'), may hold values from -0.29882812 to 0.29882812
- out_weight: bfloat16 [1024, 1024], P('shard'), may hold values from -2 to 2
- out_bias: bfloat16 [1024], P('shard'), may hold values from -0.59765625 to 0.59765625
- first_gain: bfloat16 [1024], P('shard'), may hold values from 0.5 to 1.5
- first_shift: bfloat16 [1024], P('shard'), may hold values from -0.29882812 to 0.29882812
- second_gain: bfloat16 [1024], P('shard'), may hold values from 0.5 to 1.5
- second_shift: bfloat16 [1024], P('shard'), may hold values from -3 to 3
- up_weight: bfloat16 [1024, 4096], P('shard'), may hold values from -0.1875 to 0.1875
- up_bias: bfloat16 [4096], P('shard'), may hold values from -3 to 3
- down_weight: bfloat16 [4096, 1024], P('shard'), may hold values from -0.09375 to 0.09375
- down_bias: bfloat16 [1024], P('shard'), may hold values from -3 to 3
- cotangent: bfloat16 [16, 580, 1024], P(('shard', 'rep'), 'seq'), may hold values from -6 to 6
Outputs:
- block_out: bfloat16 [16, 580, 1024], P(('shard', 'rep'), 'seq')
- token_grad: float32 [16, 580, 1024], P(('shard', 'rep'), 'seq')
- grad_qkv_weight: float32 [1024, 3072], P('shard')
- grad_query_bias: float32 [1024], P('shard')
- grad_value_bias: float32 [1024], P('shard')
- grad_out_weight: float32 [1024, 1024], P('shard')
- grad_out_bias: float32 [1024], P('shard')
- grad_first_gain: float32 [1024], P('shard')
- grad_first_shift: float32 [1024], P('shard')
- grad_second_gain: float32 [1024], P('shard')
- grad_second_shift: float32 [1024], P('shard')
- grad_up_weight: float32 [1024, 4096], P('shard')
- grad_up_bias: float32 [4096], P('shard')
- grad_down_weight: float32 [4096, 1024], P('shard')
- grad_down_bias: float32 [1024], P('shard')
The draws below stay inside these ranges and needn't reach their ends.
Inputs may be any that keep to these rules, and one draw needn't show every extreme that they name: Tokens of an image at positions lengths[image] and beyond are padding. Some image has 580 valid tokens and some has 435.
All inputs are finite; a program needn't handle non-finite values.
Results may differ from the reference program's by a relative error of at most 0.012.
Values may be sent and summed in bfloat16 or wider, within the bound.
No kernel may reach another device: no remote copies, remote signals or barrier semaphores. Data moves between devices by JAX's collectives and lax.ppermute only.
A program may use at most 192 MiB of HBM per device.

```python
from functools import partial
import jax
import jax.numpy as jnp
from jax import lax

D = 1024
H = 16
HD = 64
FF = 4096
LEN = 580
IMAGES = 16


def draw_lengths(key, part):
    removed = jax.random.randint(key, (IMAGES,), 0, LEN // 4 + 1, dtype=jnp.int32)
    removed = removed.at[0].set(0).at[1].set(LEN // 4)
    return (LEN - removed).astype(jnp.int32)


def levels(own_key, shape, cuts, low, top_value):
    level, own = 1.0, jax.random.fold_in(own_key, 6)
    for position, blocks in cuts:
        steps = jnp.exp(jax.random.uniform(jax.random.fold_in(own, position), (blocks,), jnp.float32, low / len(cuts), top_value / len(cuts)))
        level = level * jnp.repeat(steps, shape[position] // blocks).reshape([-1 if axis == position else 1 for axis in range(len(shape))])
    return level


def scatter_about(rng, extent, scale, limit, shards=(), held_as=jnp.bfloat16):
    entries = scale * jax.random.normal(rng, extent, jnp.float32)
    if shards:
        entries = entries * levels(rng, extent, shards, -0.22, 0.18)
    return jnp.clip(entries, -limit, limit).astype(held_as)


def setup_inputs(seed: int = 0) -> dict:
    streams_of = jax.random.split(jax.random.key(seed), 17)
    tokens = scatter_about(streams_of[0], (IMAGES, LEN, D), 1.0, 6.0, ((0, 16), (1, 2)))
    lengths = draw_lengths(jax.random.fold_in(streams_of[16], 71), 0)
    qkv_weight = scatter_about(streams_of[2], (D, 3 * D), D ** -0.5, 0.1875, ((0, 4),))
    query_bias = scatter_about(streams_of[3], (D,), 0.5, 3.0, ((0, 4),))
    value_bias = scatter_about(streams_of[4], (D,), 0.05, 0.29882812, ((0, 4),))
    out_weight = scatter_about(streams_of[5], (D, D), (max(1, D * 4 // LEN)) ** -0.5, 2.0, ((0, 4),))
    out_bias = scatter_about(streams_of[6], (D,), 0.1, 0.59765625, ((0, 4),))
    first_gain = jnp.clip(1.0 + 0.1 * jax.random.normal(streams_of[7], (D,), jnp.float32), 0.5, 1.5).astype(jnp.bfloat16)
    first_shift = scatter_about(streams_of[8], (D,), 0.05, 0.29882812, ((0, 4),))
    second_gain = jnp.clip(1.0 + 0.1 * jax.random.normal(streams_of[9], (D,), jnp.float32), 0.5, 1.5).astype(jnp.bfloat16)
    second_shift = scatter_about(streams_of[10], (D,), 0.5, 3.0, ((0, 4),))
    up_weight = scatter_about(streams_of[11], (D, FF), D ** -0.5, 0.1875, ((0, 4),))
    up_bias = scatter_about(streams_of[12], (FF,), 0.5, 3.0, ((0, 4),))
    down_weight = scatter_about(streams_of[13], (FF, D), FF ** -0.5, 0.09375, ((0, 4),))
    down_bias = scatter_about(streams_of[14], (D,), 0.5, 3.0, ((0, 4),))
    cotangent = scatter_about(streams_of[15], (IMAGES, LEN, D), 1.0, 6.0, ((0, 16), (1, 2)))
    return dict(tokens=tokens, lengths=lengths, qkv_weight=qkv_weight, query_bias=query_bias, value_bias=value_bias, out_weight=out_weight, out_bias=out_bias, first_gain=first_gain, first_shift=first_shift, second_gain=second_gain, second_shift=second_shift, up_weight=up_weight, up_bias=up_bias, down_weight=down_weight, down_bias=down_bias, cotangent=cotangent)


highest = lax.Precision.HIGHEST

@jax.custom_vjp
def low(v):
    return lax.optimization_barrier(v.astype(jnp.bfloat16)).astype(jnp.float32)

@jax.custom_vjp
def low_back(v):
    return v

def low_keep(v):
    return (low(v), None)

def low_pass(kept, grad):
    return (grad,)

def back_keep(v):
    return (v, None)

def back_low(kept, grad):
    return (low(grad),)
low.defvjp(low_keep, low_pass)
low_back.defvjp(back_keep, back_low)

def layer_norm(values, gain_vec, shift_vec):
    centered = values - lax.optimization_barrier(jnp.mean(values, -1, keepdims=True))
    variance = lax.optimization_barrier(jnp.mean(centered * centered, -1, keepdims=True))
    return centered * lax.rsqrt(variance + 1e-06) * gain_vec + shift_vec

def both_ways(value):
    return low(low_back(value))

def product(left, right):
    return jnp.dot(left, right, precision=highest, preferred_element_type=jnp.float32)

def attend_image(pieces):
    queries, keyset, valueset, length = pieces
    row_count = queries.shape[0]
    query_heads = queries.reshape(row_count, H, HD)
    key_heads = keyset.reshape(row_count, H, HD)
    value_heads = valueset.reshape(row_count, H, HD)
    scores = jnp.einsum('qhd,khd->hqk', query_heads, key_heads, precision=highest) * HD ** (-0.5)
    scores = low_back(scores)
    visible = jnp.arange(row_count, dtype=jnp.int32) < length
    scores = jnp.where(visible[None, None, :], scores, -1000000000.0)
    weights = low(jax.nn.softmax(scores, axis=-1))
    mixed_out = jnp.einsum('hqk,khd->qhd', weights, value_heads, precision=highest)
    return mixed_out.reshape(row_count, H * HD)

def forward(lengths, tokens, qkv_weight, query_bias, value_bias, out_weight, out_bias, first_gain, first_shift, second_gain, second_shift, up_weight, up_bias, down_weight, down_bias):
    flat_rows = tokens.reshape(-1, D)
    normed = low(layer_norm(flat_rows, first_gain, first_shift))
    projected = product(normed, qkv_weight)
    queries = both_ways(projected[:, :D] + query_bias)
    keyset = both_ways(projected[:, D:2 * D])
    valueset = both_ways(projected[:, 2 * D:] + value_bias)
    image_shape = (IMAGES, LEN, D)
    mixed_out = lax.map(jax.checkpoint(attend_image), (queries.reshape(image_shape), keyset.reshape(image_shape), valueset.reshape(image_shape), lengths))
    mixed_out = both_ways(mixed_out.reshape(-1, D))
    branch = low_back(product(mixed_out, out_weight) + out_bias)
    middle = flat_rows + branch
    second = low(layer_norm(middle, second_gain, second_shift))
    hidden = low_back(product(second, up_weight) + up_bias)
    activated = low(jax.nn.gelu(hidden, approximate=False))
    result = middle + product(activated, down_weight) + down_bias
    return result.reshape(tokens.shape)

def reference(tokens, lengths, qkv_weight, query_bias, value_bias, out_weight, out_bias, first_gain, first_shift, second_gain, second_shift, up_weight, up_bias, down_weight, down_bias, cotangent):
    params = (qkv_weight, query_bias, value_bias, out_weight, out_bias, first_gain, first_shift, second_gain, second_shift, up_weight, up_bias, down_weight, down_bias)
    params = tuple((item.astype(jnp.float32) for item in params))
    outcome, pullback = jax.vjp(partial(forward, lengths), tokens.astype(jnp.float32), *params)
    gradients = pullback(cotangent.astype(jnp.float32))
    return (outcome.astype(jnp.bfloat16), gradients[0], gradients[1], gradients[2], gradients[3], gradients[4], gradients[5], gradients[6], gradients[7], gradients[8], gradients[9], gradients[10], gradients[11], gradients[12], gradients[13])
```

```python
import functools
import math

import jax
import jax.numpy as jnp
from jax import lax
from jax.experimental import pallas as pl
from jax.experimental.pallas import tpu as pltpu
from jax.sharding import PartitionSpec as P

H = 16
HD = 64
EPS = 1e-06
F32 = jnp.float32
BF16 = jnp.bfloat16
VMEM_LIMIT = 48 * 1024 * 1024


def dims(left, right, dot_left, dot_right):
    return lax.dot_general(
        left, right, (((dot_left,), (dot_right,)), ((), ())), preferred_element_type=F32
    )


def key_visible(length_ref, padded_half, rows):
    row = lax.broadcasted_iota(jnp.int32, (2 * padded_half, 1), 0)
    second = row >= padded_half
    inside = jnp.where(second, row - padded_half, row)
    position = jnp.where(second, inside + rows, inside)
    return (inside < rows) & (position < length_ref[0])


def attend_forward(padded_half, rows, length_ref, q_ref, k_ref, v_ref, mixed_ref, log_ref):
    visible = key_visible(length_ref, padded_half, rows)
    for head in range(2):
        lanes = slice(head * HD, (head + 1) * HD)
        scores = dims(k_ref[:, lanes], q_ref[:, lanes], 1, 1) * (HD ** -0.5)
        scores = jnp.where(visible, scores, -1000000000.0)
        top = jnp.max(scores, axis=0, keepdims=True)
        shifted = jnp.exp(scores - top)
        total = jnp.sum(shifted, axis=0, keepdims=True)
        weights = (shifted * (1.0 / total)).astype(BF16)
        log_ref[0, head : head + 1, :] = top + jnp.log(total)
        values = jnp.transpose(v_ref[:, lanes].astype(F32)).astype(BF16)
        mixed = dims(values, weights, 1, 0)
        mixed_ref[:, lanes] = jnp.transpose(mixed).astype(BF16)


def attend_backward(padded_half, rows, length_ref, q_ref, k_ref, v_ref, g_ref, log_ref, out_ref):
    visible = key_visible(length_ref, padded_half, rows)
    for head in range(2):
        lanes = slice(head * HD, (head + 1) * HD)
        queries, keys = q_ref[:, lanes], k_ref[:, lanes]
        values, grads = v_ref[:, lanes], g_ref[:, lanes]
        scores = dims(keys, queries, 1, 1) * (HD ** -0.5)
        weights = jnp.where(visible, jnp.exp(scores - log_ref[0, head : head + 1, :]), 0.0)
        grad_weights = dims(values, grads, 1, 1)
        inner = jnp.sum(weights * grad_weights, axis=0, keepdims=True)
        grad_scores = (weights * (grad_weights - inner)).astype(BF16)
        keys_t = jnp.transpose(keys.astype(F32)).astype(BF16)
        grad_q = jnp.transpose(dims(keys_t, grad_scores, 1, 0)) * (HD ** -0.5)
        out_ref[0, :, lanes] = grad_q.astype(BF16)
        out_ref[1, :, lanes] = (dims(grad_scores, queries, 1, 0) * (HD ** -0.5)).astype(BF16)
        out_ref[2, :, lanes] = dims(weights.astype(BF16), grads, 1, 0).astype(BF16)


def attention(length, qkv, rows, name):
    tokens, width = qkv.shape
    pairs = width // 3 // (2 * HD)
    part = lambda p: pl.BlockSpec((tokens, 2 * HD), lambda j, n, p=p: (0, p * pairs + j))
    return pl.pallas_call(
        functools.partial(attend_forward, tokens // 2, rows),
        grid_spec=pltpu.PrefetchScalarGridSpec(
            num_scalar_prefetch=1,
            grid=(pairs,),
            in_specs=[part(0), part(1), part(2)],
            out_specs=[
                pl.BlockSpec((tokens, 2 * HD), lambda j, n: (0, j)),
                pl.BlockSpec((1, 2, tokens), lambda j, n: (j, 0, 0)),
            ],
        ),
        out_shape=[
            jax.ShapeDtypeStruct((tokens, width // 3), BF16),
            jax.ShapeDtypeStruct((pairs, 2, tokens), F32),
        ],
        compiler_params=pltpu.CompilerParams(vmem_limit_bytes=VMEM_LIMIT),
        name=name,
    )(length, qkv, qkv, qkv)


def attention_grad(length, qkv, grad_mixed, log_total, rows, name):
    tokens, width = qkv.shape
    pairs = width // 3 // (2 * HD)
    part = lambda p: pl.BlockSpec((tokens, 2 * HD), lambda j, n, p=p: (0, p * pairs + j))
    return pl.pallas_call(
        functools.partial(attend_backward, tokens // 2, rows),
        grid_spec=pltpu.PrefetchScalarGridSpec(
            num_scalar_prefetch=1,
            grid=(pairs,),
            in_specs=[
                part(0),
                part(1),
                part(2),
                pl.BlockSpec((tokens, 2 * HD), lambda j, n: (0, j)),
                pl.BlockSpec((1, 2, tokens), lambda j, n: (j, 0, 0)),
            ],
            out_specs=pl.BlockSpec((3, tokens, 2 * HD), lambda j, n: (0, 0, j)),
        ),
        out_shape=jax.ShapeDtypeStruct((3, tokens, width // 3), BF16),
        compiler_params=pltpu.CompilerParams(vmem_limit_bytes=VMEM_LIMIT),
        name=name,
    )(length, qkv, qkv, qkv, grad_mixed, log_total)


def hidden_body(x_ref, w_ref, b_ref, act_ref, slope_ref):
    hidden = dims(x_ref[...], w_ref[...], 1, 0) + b_ref[...]
    normal = 0.5 * (1.0 + lax.erf(hidden * math.sqrt(0.5)))
    density = jnp.exp(-0.5 * hidden * hidden) * (1.0 / math.sqrt(2.0 * math.pi))
    act_ref[...] = (hidden * normal).astype(BF16)
    slope_ref[...] = (normal + hidden * density).astype(BF16)


def hidden_layer(inputs, weight, bias, tile):
    tokens, depth = inputs.shape
    width = weight.shape[1]
    return pl.pallas_call(
        hidden_body,
        grid=(width // tile,),
        in_specs=[
            pl.BlockSpec((tokens, depth), lambda j: (0, 0)),
            pl.BlockSpec((depth, tile), lambda j: (0, j)),
            pl.BlockSpec((1, tile), lambda j: (0, j)),
        ],
        out_specs=[pl.BlockSpec((tokens, tile), lambda j: (0, j))] * 2,
        out_shape=[jax.ShapeDtypeStruct((tokens, width), BF16)] * 2,
        compiler_params=pltpu.CompilerParams(vmem_limit_bytes=VMEM_LIMIT),
        name="hidden_layer",
    )(inputs, weight, bias)


def weight_grad_body(count, index_ref, left_ref, right_ref, *rest):
    total = dims(left_ref[...], right_ref[...], 0, 0)
    for added in rest[:count]:
        total = total + added[...].astype(F32)
    rest[count][...] = total.astype(BF16)


def weight_grad(left, right, blocks, height, added=()):
    tokens = left.shape[0]
    number = blocks.shape[0]
    if height % 128:
        narrow = [
            lax.dynamic_slice_in_dim(left, blocks[i] * height, height, 1) for i in range(number)
        ]
        left = jnp.concatenate(narrow, axis=1)
        blocks = jnp.zeros((1,), jnp.int32)
        number, height = 1, number * height
    parts = right.shape[0] if right.ndim == 3 else 1
    width = right.shape[-1]
    if right.ndim == 3:
        right_spec = pl.BlockSpec((pl.Squeezed(), tokens, width), lambda i, j, n: (j, 0, 0))
    else:
        parts = 2
        width = width // parts
        right_spec = pl.BlockSpec((tokens, width), lambda i, j, n: (0, j))
    tile = pl.BlockSpec((height, width), lambda i, j, n: (i, j))
    return pl.pallas_call(
        functools.partial(weight_grad_body, len(added)),
        grid_spec=pltpu.PrefetchScalarGridSpec(
            num_scalar_prefetch=1,
            grid=(number, parts),
            in_specs=[pl.BlockSpec((tokens, height), lambda i, j, n: (0, n[i])), right_spec]
            + [tile] * len(added),
            out_specs=tile,
        ),
        out_shape=jax.ShapeDtypeStruct((number * height, parts * width), BF16),
        compiler_params=pltpu.CompilerParams(vmem_limit_bytes=VMEM_LIMIT),
        name="weight_grad",
    )(blocks, left, right, *added)


def normalize(values):
    centered = values - jnp.mean(values, -1, keepdims=True)
    scale = lax.rsqrt(jnp.mean(centered * centered, -1, keepdims=True) + EPS)
    return centered * scale, scale


def normalize_grad(grad, gain, normal, scale):
    scaled = grad * gain
    return scale * (
        scaled
        - jnp.mean(scaled, -1, keepdims=True)
        - normal * jnp.mean(scaled * normal, -1, keepdims=True)
    )


def place(buffer, piece, position):
    start = (position,) + (0,) * (buffer.ndim - 1)
    return lax.dynamic_update_slice(buffer, piece[None], start)


def pick(array, index, axis=0):
    return lax.dynamic_index_in_dim(array, index, axis, keepdims=False)


def shards(
    tokens,
    lengths,
    qkv_weight,
    query_bias,
    value_bias,
    out_weight,
    out_bias,
    first_gain,
    first_shift,
    second_gain,
    second_shift,
    up_weight,
    up_bias,
    down_weight,
    down_bias,
    cotangent,
):
    _, rows, width = tokens.shape
    halves = lax.axis_size("seq")
    group = lax.axis_size("shard")
    replicas = lax.axis_size("rep")
    columns = group // 2
    half, member, copy_id = (lax.axis_index(name) for name in ("seq", "shard", "rep"))
    core, column = member % 2, member // 2
    owned = width // group
    owned_hidden = up_bias.shape[0]
    padded = -(-(rows + 1) // 16) * 16

    def over_core(value):
        return lax.ppermute(value, "shard", [(i, i ^ 1) for i in range(group)])

    def over_x(value, step):
        return lax.ppermute(value, "shard", [(i, (i + 2 * step) % group) for i in range(group)])

    def over_y(value):
        return lax.ppermute(value, "seq", [(i, halves - 1 - i) for i in range(halves)])

    def over_z(value, step):
        return lax.ppermute(value, "rep", [(i, i ^ step) for i in range(replicas)])

    swaps = []
    for s in range(halves):
        for h in range(group):
            if s != h % 2:
                swaps.append((s * group + h, (h % 2) * group + (h // 2) * 2 + s))

    def swap(value):
        return lax.ppermute(value, ("seq", "shard"), swaps)

    def by_core(mine, other, axis=0):
        return jnp.where(
            core == 0, jnp.stack([mine, other], axis), jnp.stack([other, mine], axis)
        )

    def whole_image(local):
        mine = jnp.where(half == core, local, swap(local))
        return by_core(mine, over_core(mine)).reshape(2 * padded, width)

    length = lengths[0]
    lane = lax.broadcasted_iota(jnp.int32, (padded - rows, width), 1)
    note = jnp.where(lane == 0, length // 16, jnp.where(lane == 1, length % 16, 0)).astype(BF16)
    image = whole_image(jnp.concatenate([tokens[0], note], axis=0))
    grad_tail = jnp.zeros((padded - rows, width), BF16)
    image_length = image[rows, 0].astype(jnp.int32) * 16 + image[rows, 1].astype(jnp.int32)
    image_length = image_length.reshape(1)

    def gather_x(shard):
        depth = shard.shape[0]
        split = shard.reshape((halves, depth // halves) + shard.shape[1:])
        buffer = jnp.zeros((columns * halves,) + split.shape[1:], shard.dtype)
        buffer = lax.dynamic_update_slice(
            buffer, split, (column * halves,) + (0,) * (split.ndim - 1)
        )
        first = pick(split, half)
        for step in range(1, columns):
            source = (column - step) % columns
            got = over_x(first, step)
            buffer = place(buffer, got, source * halves + half)
            buffer = place(buffer, over_y(got), source * halves + (halves - 1 - half))
        return buffer.reshape((columns, depth) + shard.shape[1:])

    def by_columns(gathered, blocks):
        depth, wide = gathered.shape[1:]
        one = wide // blocks // columns // 2
        cut = [
            jnp.concatenate(
                [
                    gathered[:, :, (2 * k + i) * one : (2 * k + i + 1) * one]
                    for k in range(blocks * columns)
                ],
                axis=2,
            )
            for i in range(2)
        ]
        keep = jnp.where(core == 0, cut[0], cut[1])
        send = jnp.where(core == 0, cut[1], cut[0])
        return by_core(keep, over_core(send), 1).reshape(columns * 2 * depth, wide // 2)

    vectors = jnp.concatenate(
        [
            query_bias,
            value_bias,
            out_bias,
            first_gain,
            first_shift,
            second_gain,
            second_shift,
            down_bias,
            up_bias,
        ]
    ).reshape(-1, 128)
    gathered_vec = jnp.zeros((columns,) + vectors.shape, BF16)
    gathered_vec = place(gathered_vec, vectors, column)
    for step in range(1, columns):
        gathered_vec = place(gathered_vec, over_x(vectors, step), (column - step) % columns)
    mine_vec = gathered_vec.reshape(columns, -1).astype(F32)
    all_vec = by_core(gathered_vec, over_core(gathered_vec), 1).reshape(columns * 2, -1)
    all_vec = all_vec.astype(F32)
    vec = lambda i: all_vec[:, i * owned : (i + 1) * owned].reshape(width)
    own_vec = lambda i: mine_vec[:, i * owned : (i + 1) * owned].reshape(width // 2)
    gain_one, shift_one, gain_two, shift_two = vec(3), vec(4), vec(5), vec(6)
    vec_out, vec_down = vec(2), vec(7)
    vec_up = mine_vec[:, 8 * owned :].reshape(1, columns * owned_hidden)
    vec_qkv = jnp.concatenate([own_vec(0), jnp.zeros((width // 2,), F32), own_vec(1)])

    wqkv = by_columns(gather_x(qkv_weight), 3)
    wout = gather_x(out_weight).reshape(width // 2, width)
    wup = by_columns(gather_x(up_weight), 1)
    wdown = gather_x(down_weight).reshape(columns * owned_hidden, width)
    incoming = whole_image(jnp.concatenate([cotangent[0], grad_tail], axis=0))

    image_f = image.astype(F32)
    normal_one, scale_one = normalize(image_f)
    first_low = (normal_one * gain_one + shift_one).astype(BF16)
    qkv = (jnp.dot(first_low, wqkv, preferred_element_type=F32) + vec_qkv).astype(BF16)
    mixed, log_total = attention(image_length, qkv, rows, "attention")
    branch = jnp.dot(mixed, wout, preferred_element_type=F32)
    middle = image_f + branch + over_core(branch.astype(BF16)).astype(F32) + vec_out
    normal_two, scale_two = normalize(middle)
    second_low = (normal_two * gain_two + shift_two).astype(BF16)
    act_low, slope = hidden_layer(second_low, wup, vec_up, 512)

    grad_act = jnp.dot(incoming, wdown.T, preferred_element_type=F32)
    hidden_low = (grad_act * slope.astype(F32)).astype(BF16)
    grad_second = jnp.dot(hidden_low, wup.T, preferred_element_type=F32)
    grad_second = grad_second + over_core(grad_second.astype(BF16)).astype(F32)
    incoming_f = incoming.astype(F32)
    grad_middle = incoming_f + normalize_grad(grad_second, gain_two, normal_two, scale_two)
    branch_low = grad_middle.astype(BF16)
    grad_mixed = jnp.dot(branch_low, wout.T, preferred_element_type=F32).astype(BF16)
    grad_qkv = attention_grad(image_length, qkv, grad_mixed, log_total, rows, "attention_grad")
    flat_grad = jnp.concatenate([grad_qkv[0], grad_qkv[1], grad_qkv[2]], axis=1)
    grad_first = jnp.dot(flat_grad, wqkv.T, preferred_element_type=F32)
    grad_first = grad_first + over_core(grad_first.astype(BF16)).astype(F32)
    token_grad = grad_middle + normalize_grad(grad_first, gain_one, normal_one, scale_one)

    partial = jnp.dot(act_low, wdown, preferred_element_type=F32).reshape(2, padded, width)
    from_other = over_core(pick(partial, 1 - core).astype(BF16)).astype(F32)
    own_middle = pick(middle.reshape(2, padded, width), core)
    block = (own_middle + pick(partial, core) + from_other + vec_down).astype(BF16)
    block = jnp.where(half == core, block, swap(block))
    block_out = block[:rows][None]
    own_grad = pick(token_grad.reshape(2, padded, width), core)
    moved = swap(own_grad.astype(BF16)).astype(F32)
    token_grad = jnp.where(half == core, own_grad, moved)[:rows][None]

    mine = lambda v: pick(v.reshape(columns, 2, owned), core, 1)
    summed = lambda v: jnp.sum(v, 0)
    vec_grads = jnp.concatenate(
        [
            summed(grad_qkv[0].astype(F32)).reshape(columns, owned),
            summed(grad_qkv[2].astype(F32)).reshape(columns, owned),
            mine(summed(branch_low.astype(F32))),
            mine(summed(grad_first * normal_one)),
            mine(summed(grad_first)),
            mine(summed(grad_second * normal_two)),
            mine(summed(grad_second)),
            mine(summed(incoming_f)),
            summed(hidden_low.astype(F32)).reshape(columns, owned_hidden),
        ],
        axis=1,
    )
    entries = vec_grads.shape[1]
    pieces = halves * replicas
    vec_grads = vec_grads.reshape(columns, halves, replicas, 1, entries // pieces)
    vec_grads = jnp.pad(
        vec_grads, ((0, 0), (0, 0), (0, 0), (0, 7), (0, width - entries // pieces))
    ).astype(BF16)

    def reduce_all(quadrant, lead, cross):
        other = halves - 1 - half
        sent = [quadrant((column + k) % columns, other, ()) for k in range(1, columns)]
        got = [over_x(v, k + 1) for k, v in enumerate(sent)]
        sent_b = [quadrant((column + k) % columns, half, ()) for k in range(1, columns)]
        got_b = [over_x(v, k + 1) for k, v in enumerate(sent_b)]
        from_y = over_y(quadrant(column, other, tuple(got)))
        total = quadrant(column, half, tuple(got_b) + (from_y,))
        total = total.reshape((lead, replicas, total.shape[0] // lead // replicas, total.shape[1]))
        step = 1
        while step < replicas:
            bit = (copy_id // step) % 2
            pairs = total.reshape((lead, total.shape[1] // 2, 2) + total.shape[2:])
            got = over_z(pick(pairs, 1 - bit, 2), step)
            total = (pick(pairs, bit, 2).astype(F32) + got.astype(F32)).astype(BF16)
            step *= 2
        total = total.reshape((lead,) + total.shape[2:])
        if cross:
            total = cross(total)
        else:
            total = total[0]
        total = total[None]
        while step > 1:
            step //= 2
            bit = (copy_id // step) % 2
            got = over_z(total, step)
            total = jnp.where(
                bit == 0, jnp.stack([total, got], 1), jnp.stack([got, total], 1)
            ).reshape((-1,) + total.shape[1:])
        got = over_y(total)
        return jnp.where(
            half == 0, jnp.stack([total, got], 0), jnp.stack([got, total], 0)
        )

    def cross_cores(blocks):
        def exchange(total):
            got = over_core(pick(total, 1 - core))
            own = pick(total, core)
            one = own.shape[1] // blocks
            left = jnp.where(core == 0, own, got)
            right = jnp.where(core == 0, got, own)
            cols = []
            for k in range(blocks):
                cols += [left[:, k * one : (k + 1) * one], right[:, k * one : (k + 1) * one]]
            return jnp.concatenate(cols, axis=1)

        return exchange

    def by_row(left, right):
        height = owned // halves

        def quadrant(x, y, added):
            blocks = jnp.stack([(x * 2 + i) * halves + y for i in range(2)]).astype(jnp.int32)
            return weight_grad(left, right, blocks, height, added)

        return quadrant

    def by_own(left, right, height):
        def quadrant(x, y, added):
            blocks = (x * halves + y).astype(jnp.int32).reshape(1)
            return weight_grad(left, right, blocks, height, added)

        return quadrant

    def out_quadrant(x, y, added):
        height = owned // halves
        blocks = (x * halves + y).astype(jnp.int32).reshape(1)
        core_part = weight_grad(mixed, branch_low, blocks, height)
        core_part = core_part.reshape(replicas, height // replicas, width)
        joined = jnp.concatenate([core_part, pick(pick(vec_grads, x), y)], axis=1)
        joined = joined.reshape(-1, width).astype(F32)
        for value in added:
            joined = joined + value.astype(F32)
        return joined.astype(BF16)

    grad_down = reduce_all(by_own(act_low, incoming, owned_hidden // halves), 1, None)
    grad_up = reduce_all(by_row(second_low, hidden_low), 2, cross_cores(columns))
    grad_qkv_w = reduce_all(by_row(first_low, grad_qkv), 2, cross_cores(3 * columns))
    grad_out = reduce_all(out_quadrant, 1, None)

    height = owned // pieces
    vec_out_grads = grad_out[:, :, height, : entries // pieces].astype(F32).reshape(entries)
    vec_of = lambda i: vec_out_grads[i * owned : (i + 1) * owned]
    grad_out = grad_out[:, :, :height].astype(F32).reshape(owned, width)
    return (
        block_out,
        token_grad,
        grad_qkv_w.astype(F32).reshape(owned, 3 * width),
        vec_of(0),
        vec_of(1),
        grad_out,
        vec_of(2),
        vec_of(3),
        vec_of(4),
        vec_of(5),
        vec_of(6),
        grad_up.astype(F32).reshape(owned, up_weight.shape[1]),
        vec_out_grads[8 * owned :],
        grad_down.astype(F32).reshape(owned_hidden, width),
        vec_of(7),
    )


def solution(mesh):
    return jax.shard_map(
        shards,
        mesh=mesh,
        in_specs=(
            P(("shard", "rep"), "seq", None),
            P(("shard", "rep")),
            P("shard", None),
            P("shard"),
            P("shard"),
            P("shard", None),
            P("shard"),
            P("shard"),
            P("shard"),
            P("shard"),
            P("shard"),
            P("shard", None),
            P("shard"),
            P("shard", None),
            P("shard"),
            P(("shard", "rep"), "seq", None),
        ),
        out_specs=(
            P(("shard", "rep"), "seq", None),
            P(("shard", "rep"), "seq", None),
            P("shard", None),
            P("shard"),
            P("shard"),
            P("shard", None),
            P("shard"),
            P("shard"),
            P("shard"),
            P("shard"),
            P("shard"),
            P("shard", None),
            P("shard"),
            P("shard", None),
            P("shard"),
        ),
        check_vma=False,
    )
```

```python
import functools
import math

import jax
import jax.numpy as jnp
from jax import lax
from jax.experimental import pallas as pl
from jax.experimental.pallas import tpu as pltpu
from jax.sharding import PartitionSpec as P

H = 16
HD = 64
EPS = 1e-06
F32 = jnp.float32
BF16 = jnp.bfloat16
VMEM_LIMIT = 48 * 1024 * 1024


def dims(left, right, dot_left, dot_right):
    return lax.dot_general(
        left, right, (((dot_left,), (dot_right,)), ((), ())), preferred_element_type=F32
    )


def whole(*shape):
    return pl.BlockSpec(shape, lambda *index: (0,) * len(shape))


def run(body, name, grid, place, operands, in_specs, outs, scratch=()):
    return pl.pallas_call(
        body,
        grid_spec=pltpu.PrefetchScalarGridSpec(
            num_scalar_prefetch=1,
            grid=grid,
            in_specs=in_specs,
            out_specs=[out[2] for out in outs],
            scratch_shapes=list(scratch),
        ),
        out_shape=[jax.ShapeDtypeStruct(out[0], out[1]) for out in outs],
        compiler_params=pltpu.CompilerParams(vmem_limit_bytes=VMEM_LIMIT),
        name=name,
    )(place, *operands)


def numbers(*values):
    return jnp.stack([jnp.asarray(value, jnp.int32) for value in values])


def key_visible(note_ref, padded_half, rows):
    note = note_ref[...].astype(F32)[rows % 16 : rows % 16 + 1, :]
    length = note[:, 0:1] * 16.0 + note[:, 1:2]
    row = lax.broadcasted_iota(jnp.int32, (2 * padded_half, 1), 0)
    second = row >= padded_half
    inside = jnp.where(second, row - padded_half, row)
    position = jnp.where(second, inside + rows, inside)
    return (inside < rows) & (position.astype(F32) < length)


def attend_forward(padded_half, rows, place_ref, note_ref, q_ref, k_ref, v_ref, mixed_ref, log_ref):
    visible = key_visible(note_ref, padded_half, rows)
    for head in range(2):
        lanes = slice(head * HD, (head + 1) * HD)
        scores = dims(k_ref[:, lanes], q_ref[:, lanes], 1, 1) * (HD ** -0.5)
        scores = jnp.where(visible, scores, -1000000000.0)
        top = jnp.max(scores, axis=0, keepdims=True)
        shifted = jnp.exp(scores - top)
        total = jnp.sum(shifted, axis=0, keepdims=True)
        weights = (shifted * (1.0 / total)).astype(BF16)
        log_ref[0, head : head + 1, :] = top + jnp.log(total)
        values = jnp.transpose(v_ref[:, lanes].astype(F32)).astype(BF16)
        mixed = dims(values, weights, 1, 0)
        mixed_ref[:, lanes] = jnp.transpose(mixed).astype(BF16)


def attend_backward(
    padded_half, rows, place_ref, note_ref, q_ref, k_ref, v_ref, g_ref, log_ref, out_ref, sum_ref
):
    visible = key_visible(note_ref, padded_half, rows)
    for head in range(2):
        lanes = slice(head * HD, (head + 1) * HD)
        queries, keys = q_ref[:, lanes], k_ref[:, lanes]
        values, grads = v_ref[:, lanes], g_ref[:, lanes]
        scores = dims(keys, queries, 1, 1) * (HD ** -0.5)
        weights = jnp.where(visible, jnp.exp(scores - log_ref[0, head : head + 1, :]), 0.0)
        grad_weights = dims(values, grads, 1, 1)
        inner = jnp.sum(weights * grad_weights, axis=0, keepdims=True)
        grad_scores = (weights * (grad_weights - inner)).astype(BF16)
        keys_t = jnp.transpose(keys.astype(F32)).astype(BF16)
        grad_q = (jnp.transpose(dims(keys_t, grad_scores, 1, 0)) * (HD ** -0.5)).astype(BF16)
        grad_v = dims(weights.astype(BF16), grads, 1, 0).astype(BF16)
        out_ref[0, :, lanes] = grad_q
        out_ref[1, :, lanes] = (dims(grad_scores, queries, 1, 0) * (HD ** -0.5)).astype(BF16)
        out_ref[2, :, lanes] = grad_v
        sum_ref[0, 0:1, lanes] = jnp.sum(grad_q.astype(F32), axis=0, keepdims=True)
        sum_ref[0, 1:2, lanes] = jnp.sum(grad_v.astype(F32), axis=0, keepdims=True)


def attention(place, image, qkv, rows):
    tokens, width = qkv.shape
    pairs = width // 3 // (2 * HD)
    part = lambda p: pl.BlockSpec((tokens, 2 * HD), lambda j, n, p=p: (0, p * pairs + j))
    return run(
        functools.partial(attend_forward, tokens // 2, rows),
        "attention",
        (pairs,),
        place,
        (image, qkv, qkv, qkv),
        [pl.BlockSpec((16, 128), lambda j, n: (rows // 16, 0)), part(0), part(1), part(2)],
        [
            ((tokens, width // 3), BF16, pl.BlockSpec((tokens, 2 * HD), lambda j, n: (0, j))),
            ((pairs, 2, tokens), F32, pl.BlockSpec((1, 2, tokens), lambda j, n: (j, 0, 0))),
        ],
    )


def attention_grad(place, image, qkv, grad_mixed, log_total, rows):
    tokens, width = qkv.shape
    pairs = width // 3 // (2 * HD)
    part = lambda p: pl.BlockSpec((tokens, 2 * HD), lambda j, n, p=p: (0, p * pairs + j))
    return run(
        functools.partial(attend_backward, tokens // 2, rows),
        "attention_grad",
        (pairs,),
        place,
        (image, qkv, qkv, qkv, grad_mixed, log_total),
        [
            pl.BlockSpec((16, 128), lambda j, n: (rows // 16, 0)),
            part(0),
            part(1),
            part(2),
            pl.BlockSpec((tokens, 2 * HD), lambda j, n: (0, j)),
            pl.BlockSpec((1, 2, tokens), lambda j, n: (j, 0, 0)),
        ],
        [
            (
                (3, tokens, width // 3),
                BF16,
                pl.BlockSpec((3, tokens, 2 * HD), lambda j, n: (0, 0, j)),
            ),
            ((pairs, 8, 2 * HD), F32, pl.BlockSpec((1, 8, 2 * HD), lambda j, n: (j, 0, 0))),
        ],
    )


def norm_one_body(place_ref, own_ref, other_ref, gain_ref, shift_ref, image_ref, low_ref):
    def write(values_ref):
        normal, _ = normalize(values_ref[...].astype(F32))
        image_ref[...] = values_ref[...]
        low_ref[...] = (normal * gain_ref[...] + shift_ref[...]).astype(BF16)

    mine = pl.program_id(0) == place_ref[0]
    pl.when(mine)(lambda: write(own_ref))
    pl.when(jnp.logical_not(mine))(lambda: write(other_ref))


def norm_one(place, own, other, gain, shift):
    padded, width = own.shape
    rows = pl.BlockSpec((padded, width), lambda i, n: (i, 0))
    shape = (2 * padded, width)
    return run(
        norm_one_body,
        "norm_one",
        (2,),
        place,
        (own, other, gain, shift),
        [whole(padded, width)] * 2 + [whole(1, width)] * 2,
        [(shape, BF16, rows)] * 2,
    )


def norm_two_body(
    place_ref, image_ref, own_ref, other_ref, bias_ref, gain_ref, shift_ref, middle_ref, low_ref
):
    branch = own_ref[...].astype(F32) + other_ref[...].astype(F32)
    middle = image_ref[...].astype(F32) + branch + bias_ref[...]
    normal, _ = normalize(middle)
    middle_ref[...] = middle
    low_ref[...] = (normal * gain_ref[...] + shift_ref[...]).astype(BF16)


def norm_two(place, image, own, other, bias, gain, shift):
    tokens, width = image.shape
    rows = pl.BlockSpec((tokens // 2, width), lambda i, n: (i, 0))
    return run(
        norm_two_body,
        "norm_two",
        (2,),
        place,
        (image, own, other, bias, gain, shift),
        [rows] * 3 + [whole(1, width)] * 3,
        [((tokens, width), F32, rows), ((tokens, width), BF16, rows)],
    )


def add_sums(sum_ref, values):
    @pl.when(pl.program_id(0) == 0)
    def _():
        sum_ref[...] = jnp.zeros_like(sum_ref)

    for k, value in enumerate(values):
        sum_ref[k : k + 1, :] += jnp.sum(value, axis=0, keepdims=True)


def norm_two_back_body(
    place_ref, incoming_ref, own_ref, other_ref, middle_ref, gain_ref, grad_ref, low_ref, sum_ref
):
    incoming = incoming_ref[...].astype(F32)
    grad = own_ref[...].astype(F32) + other_ref[...].astype(F32)
    normal, scale = normalize(middle_ref[...])
    grad_middle = incoming + normalize_grad(grad, gain_ref[...], normal, scale)
    low = grad_middle.astype(BF16)
    grad_ref[...] = grad_middle
    low_ref[...] = low
    add_sums(sum_ref, (grad * normal, grad, low.astype(F32), incoming))


def norm_two_back(place, incoming, own, other, middle, gain):
    tokens, width = incoming.shape
    rows = pl.BlockSpec((tokens // 2, width), lambda i, n: (i, 0))
    return run(
        norm_two_back_body,
        "norm_two_back",
        (2,),
        place,
        (incoming, own, other, middle, gain),
        [rows] * 4 + [whole(1, width)],
        [((tokens, width), F32, rows), ((tokens, width), BF16, rows), ((8, width), F32, whole(8, width))],
    )


def norm_one_back_body(
    place_ref, grad_ref, own_ref, other_ref, image_ref, gain_ref, kept_ref, low_ref, sum_ref
):
    grad = own_ref[...].astype(F32) + other_ref[...].astype(F32)
    normal, scale = normalize(image_ref[...].astype(F32))
    total = grad_ref[...] + normalize_grad(grad, gain_ref[...], normal, scale)
    add_sums(sum_ref, (grad * normal, grad))

    @pl.when(pl.program_id(0) == place_ref[0])
    def _():
        kept_ref[...] = total
        low_ref[...] = total.astype(BF16)


def norm_one_back(place, grad_middle, own, other, image, gain):
    tokens, width = image.shape
    padded = tokens // 2
    rows = pl.BlockSpec((padded, width), lambda i, n: (i, 0))
    return run(
        norm_one_back_body,
        "norm_one_back",
        (2,),
        place,
        (grad_middle, own, other, image, gain),
        [rows] * 4 + [whole(1, width)],
        [
            ((padded, width), F32, whole(padded, width)),
            ((padded, width), BF16, whole(padded, width)),
            ((8, width), F32, whole(8, width)),
        ],
    )


def split_body(part_rows, place_ref, keep_in, send_in, keep, send, *parts):
    keep[...] = keep_in[...]
    send[...] = send_in[...]
    if parts:
        first = pl.multiple_of(place_ref[1] * part_rows, part_rows)
        parts[0][...] = keep_in[pl.ds(first, part_rows), :]
        parts[1][...] = send_in[pl.ds(first, part_rows), :]


def split_columns(place, shard, number, part_rows, name):
    depth, wide = shard.shape
    one = wide // number // 2
    out = lambda rows: ((rows, wide // 2), BF16, pl.BlockSpec((rows, one), lambda j, n: (0, j)))
    return run(
        functools.partial(split_body, part_rows),
        name,
        (number,),
        place,
        (shard, shard),
        [
            pl.BlockSpec((depth, one), lambda j, n: (0, 2 * j + n[0])),
            pl.BlockSpec((depth, one), lambda j, n: (0, 2 * j + 1 - n[0])),
        ],
        [out(depth)] * 2 + ([out(part_rows)] * 2 if part_rows else []),
    )


def pair_body(rows, place_ref, own_ref, other_ref, out_ref):
    first = pl.multiple_of(place_ref[1] * rows, rows)
    zero = place_ref[0] == 0
    own, other = own_ref[pl.ds(first, rows), :], other_ref[pl.ds(first, rows), :]
    out_ref[:rows, :] = jnp.where(zero, own, other)
    out_ref[rows:, :] = jnp.where(zero, other, own)


def pair_part(place, own, other, rows):
    depth, wide = own.shape
    tile = wide // 2
    return run(
        functools.partial(pair_body, rows),
        "pair_part",
        (2,),
        place,
        (own, other),
        [pl.BlockSpec((depth, tile), lambda j, n: (0, j))] * 2,
        [((2 * rows, wide), BF16, pl.BlockSpec((2 * rows, tile), lambda j, n: (0, j)))],
    )[0]


def join_body(blocks, count, finish, place_ref, left_ref, bias_ref, *refs):
    pieces, joined_ref, outs = refs[:count], refs[count], refs[count + 1 :]
    for k, (number, source, rows) in enumerate(blocks):
        first = pl.multiple_of(place_ref[k] * rows, rows)
        joined_ref[pl.ds(first, rows), :] = pieces[number][source : source + rows, :]
    total = dims(left_ref[...], joined_ref[...], 1, 0) + bias_ref[...]
    for out, value in zip(outs, finish(total)):
        out[...] = value.astype(out.dtype)


def join_dot(line, left, pieces, bias, finish, results, tile, name):
    arrays = []
    for piece in pieces:
        if not any(piece[0] is array for array in arrays):
            arrays.append(piece[0])
    number = lambda array: [array is other for other in arrays].index(True)
    blocks = [(number(array), source, rows) for array, source, rows, _ in pieces]
    place = line.gate(numbers(*[piece[3] for piece in pieces]))
    tokens, depth = left.shape
    wide = arrays[0].shape[1]
    spec = lambda rows: pl.BlockSpec((rows, tile), lambda j, n: (0, j))
    return line.mark(
        run(
            functools.partial(join_body, blocks, len(arrays), finish),
            name,
            (wide // tile,),
            place,
            (left, bias) + tuple(arrays),
            [whole(tokens, depth), spec(1)] + [spec(array.shape[0]) for array in arrays],
            [((depth, wide), BF16, spec(depth))] + [((tokens, wide), BF16, spec(tokens))] * results,
        )
    )


def activate(hidden):
    normal = 0.5 * (1.0 + lax.erf(hidden * math.sqrt(0.5)))
    density = jnp.exp(-0.5 * hidden * hidden) * (1.0 / math.sqrt(2.0 * math.pi))
    return hidden * normal, normal + hidden * density


def feed_back_body(
    own_blocks, count, place_ref, incoming_ref, act_ref, slope_ref, own_ref, *refs
):
    others, (low_ref, sum_ref, part_ref), (weight_ref, total_ref) = (
        refs[:count],
        refs[count : count + 3],
        refs[count + 3 :],
    )
    step = pl.program_id(0)

    @pl.when(step < own_blocks)
    def _():
        weight_ref[...] = own_ref[...]

    for k in range(count):

        @pl.when(step == own_blocks + k)
        def _(k=k):
            weight_ref[...] = others[k][...]

    grad = dims(incoming_ref[...], weight_ref[...], 1, 1) * slope_ref[...].astype(F32)
    low = grad.astype(BF16)
    low_ref[...] = low
    sum_ref[...] = jnp.sum(low.astype(F32), axis=0, keepdims=True)
    part = dims(act_ref[...], weight_ref[...], 1, 0)
    total = jnp.where(step == 0, part, total_ref[...] + part)
    total_ref[...] = total

    @pl.when(step == own_blocks + count - 1)
    def _():
        part_ref[...] = total.astype(BF16)


def feed_back(place, incoming, act, slope, own, others):
    tokens, width = incoming.shape
    hidden = act.shape[1]
    tile = others[0].shape[0]
    own_blocks = own.shape[0] // tile
    steps = own_blocks + len(others)
    block = pl.BlockSpec((tokens, tile), lambda s, n: (0, n[s]))
    return run(
        functools.partial(feed_back_body, own_blocks, len(others)),
        "feed_back",
        (steps,),
        place,
        (incoming, act, slope, own) + tuple(others),
        [
            whole(tokens, width),
            block,
            block,
            pl.BlockSpec((tile, width), lambda s, n: (jnp.minimum(s, own_blocks - 1), 0)),
        ]
        + [whole(tile, width)] * len(others),
        [
            ((tokens, hidden), BF16, block),
            ((1, hidden), F32, pl.BlockSpec((1, tile), lambda s, n: (0, n[s]))),
            ((tokens, width), BF16, whole(tokens, width)),
        ],
        [pltpu.VMEM((tile, width), BF16), pltpu.VMEM((tokens, width), F32)],
    )


def dot_rows_body(place_ref, left_ref, weight_ref, out_ref):
    parts = left_ref.shape[0] if len(left_ref.shape) == 3 else 1
    if parts == 1:
        total = dims(left_ref[...], weight_ref[...], 1, 1)
    else:
        one = left_ref.shape[2]
        total = dims(left_ref[0], weight_ref[:, :one], 1, 1)
        for p in range(1, parts):
            total = total + dims(left_ref[p], weight_ref[:, p * one : (p + 1) * one], 1, 1)
    out_ref[...] = total.astype(BF16)


def dot_rows(place, left, weight, tile, name):
    tokens = left.shape[-2]
    rows, depth = weight.shape
    return run(
        dot_rows_body,
        name,
        (rows // tile,),
        place,
        (left, weight),
        [whole(*left.shape), pl.BlockSpec((tile, depth), lambda j, n: (j, 0))],
        [((tokens, rows), BF16, pl.BlockSpec((tokens, tile), lambda j, n: (0, j)))],
    )[0]


def pack_body(columns, owned, replicas, share, place_ref, two_ref, one_ref, qv_ref, up_ref, out_ref):
    zero = place_ref[0] == 0
    pairs = qv_ref.shape[0] // columns
    hidden = up_ref.shape[1] // columns
    out_ref[...] = jnp.zeros_like(out_ref)
    for x in range(columns):
        parts = [qv_ref[x * pairs + p, row : row + 1, :] for row in range(2) for p in range(pairs)]
        for ref, row in ((two_ref, 2), (one_ref, 0), (one_ref, 1), (two_ref, 0), (two_ref, 1), (two_ref, 3)):
            first, second = (
                ref[row : row + 1, (2 * x + c) * owned : (2 * x + c + 1) * owned] for c in range(2)
            )
            parts.append(jnp.where(zero, first, second))
        parts.append(up_ref[:, x * hidden : (x + 1) * hidden])
        row = jnp.concatenate(parts, axis=1)
        for p in range(out_ref.shape[1] // 8):
            out_ref[x, 8 * p : 8 * p + 1, :share] = row[:, p * share : (p + 1) * share]


def out_grad_body(count, replicas, place_ref, left_ref, right_ref, vec_ref, *rest):
    total = dims(left_ref[...], right_ref[...], 0, 0)
    height = total.shape[0] // replicas
    every = height + 8
    for z in range(replicas):
        for first, value in (
            (z * every, total[z * height : (z + 1) * height]),
            (z * every + height, vec_ref[0, 8 * z : 8 * z + 8, :]),
        ):
            rows = slice(first, first + value.shape[0])
            for added in rest[:count]:
                value = value + added[rows, :].astype(F32)
            rest[count][rows, :] = value.astype(BF16)


def out_grad(place, left, right, vectors, height, replicas, added=()):
    tokens, width = right.shape
    every = height + 8 * replicas
    if height % 128:
        left = lax.dynamic_slice_in_dim(left, place[0] * height, height, 1)
        place = place * numbers(0, 1, 1)
    return run(
        functools.partial(out_grad_body, len(added), replicas),
        "out_grad",
        (1,),
        place,
        (left, right, vectors) + tuple(added),
        [
            pl.BlockSpec((tokens, height), lambda i, n: (0, n[0])),
            whole(tokens, width),
            pl.BlockSpec((1, 8 * replicas, width), lambda i, n: (n[1], n[2], 0)),
        ]
        + [whole(every, width)] * len(added),
        [((every, width), BF16, whole(every, width))],
    )[0]


def weight_grad_body(count, index_ref, left_ref, right_ref, *rest):
    total = dims(left_ref[...], right_ref[...], 0, 0)
    for added in rest[:count]:
        total = total + added[...].astype(F32)
    rest[count][...] = total.astype(BF16)


def weight_grad(left, right, blocks, height, added=()):
    tokens = left.shape[0]
    number = blocks.shape[0]
    if height % 128:
        narrow = [
            lax.dynamic_slice_in_dim(left, blocks[i] * height, height, 1) for i in range(number)
        ]
        left = jnp.concatenate(narrow, axis=1)
        blocks = jnp.zeros((1,), jnp.int32)
        number, height = 1, number * height
    parts = right.shape[0] if right.ndim == 3 else 1
    width = right.shape[-1]
    if right.ndim == 3:
        right_spec = pl.BlockSpec((pl.Squeezed(), tokens, width), lambda i, j, n: (j, 0, 0))
    else:
        parts = 2
        width = width // parts
        right_spec = pl.BlockSpec((tokens, width), lambda i, j, n: (0, j))
    tile = pl.BlockSpec((height, width), lambda i, j, n: (i, j))
    return pl.pallas_call(
        functools.partial(weight_grad_body, len(added)),
        grid_spec=pltpu.PrefetchScalarGridSpec(
            num_scalar_prefetch=1,
            grid=(number, parts),
            in_specs=[pl.BlockSpec((tokens, height), lambda i, j, n: (0, n[i])), right_spec]
            + [tile] * len(added),
            out_specs=tile,
        ),
        out_shape=jax.ShapeDtypeStruct((number * height, parts * width), BF16),
        compiler_params=pltpu.CompilerParams(vmem_limit_bytes=VMEM_LIMIT),
        name="weight_grad",
    )(blocks, left, right, *added)


class Line:
    def __init__(self):
        self.last = None

    def gate(self, value):
        if self.last is None:
            return value
        return lax.optimization_barrier((value, self.last))[0]

    def mark(self, value):
        self.last = value
        return value

    def pass_on(self, value):
        return self.mark(self.gate(value))


def normalize(values):
    centered = values - jnp.mean(values, -1, keepdims=True)
    scale = lax.rsqrt(jnp.mean(centered * centered, -1, keepdims=True) + EPS)
    return centered * scale, scale


def normalize_grad(grad, gain, normal, scale):
    scaled = grad * gain
    return scale * (
        scaled
        - jnp.mean(scaled, -1, keepdims=True)
        - normal * jnp.mean(scaled * normal, -1, keepdims=True)
    )


def place(buffer, piece, position):
    start = (position,) + (0,) * (buffer.ndim - 1)
    return lax.dynamic_update_slice(buffer, piece[None], start)


def pick(array, index, axis=0):
    return lax.dynamic_index_in_dim(array, index, axis, keepdims=False)


def shards(
    tokens,
    lengths,
    qkv_weight,
    query_bias,
    value_bias,
    out_weight,
    out_bias,
    first_gain,
    first_shift,
    second_gain,
    second_shift,
    up_weight,
    up_bias,
    down_weight,
    down_bias,
    cotangent,
):
    _, rows, width = tokens.shape
    halves = lax.axis_size("seq")
    group = lax.axis_size("shard")
    replicas = lax.axis_size("rep")
    columns = group // 2
    half, member, copy_id = (lax.axis_index(name) for name in ("seq", "shard", "rep"))
    core, column = member % 2, member // 2
    owned = width // group
    owned_hidden = up_bias.shape[0]
    padded = -(-(rows + 1) // 16) * 16

    def over_core(value):
        return lax.ppermute(value, "shard", [(i, i ^ 1) for i in range(group)])

    def over_x(value, step):
        return lax.ppermute(value, "shard", [(i, (i + 2 * step) % group) for i in range(group)])

    def over_x_core(value, step):
        pairs = [(i, ((i + 2 * step) % group) ^ 1) for i in range(group)]
        return lax.ppermute(value, "shard", pairs)

    def over_y(value):
        return lax.ppermute(value, "seq", [(i, halves - 1 - i) for i in range(halves)])

    def over_z(value, step):
        return lax.ppermute(value, "rep", [(i, i ^ step) for i in range(replicas)])

    swaps = []
    for s in range(halves):
        for h in range(group):
            if s != h % 2:
                swaps.append((s * group + h, (h % 2) * group + (h // 2) * 2 + s))

    def swap(value):
        return lax.ppermute(value, ("seq", "shard"), swaps)

    def by_core(mine, other, axis=0):
        return jnp.where(
            core == 0, jnp.stack([mine, other], axis), jnp.stack([other, mine], axis)
        )

    line = Line()
    steps = range(1, columns)
    other_half = halves - 1 - half
    side = copy_id % 2
    quarter = half * 2 + side

    length = lengths[0]
    lane = lax.broadcasted_iota(jnp.int32, (padded - rows, width), 1)
    note = jnp.where(lane == 0, length // 16, jnp.where(lane == 1, length % 16, 0)).astype(BF16)
    own_tokens = line.mark(jnp.concatenate([tokens[0], note], axis=0))
    other_tokens = swap(own_tokens)

    qkv_keep, qkv_send, qkv_part, qkv_cross = line.mark(
        split_columns(
            line.gate(numbers(core, half)), qkv_weight, 3 * columns, owned // halves, "split_qkv"
        )
    )
    qkv_x = [(over_x(qkv_part, k), over_x_core(qkv_cross, k)) for k in steps]
    qkv_core = over_core(qkv_send)

    vectors = jnp.concatenate(
        [
            line.gate(query_bias),
            value_bias,
            out_bias,
            first_gain,
            first_shift,
            second_gain,
            second_shift,
            down_bias,
            up_bias,
        ]
    ).reshape(-1, 128)
    line.mark(vectors)
    vec_x = [over_x(vectors, k) for k in steps]

    own_half = lambda shard: pick(
        shard.reshape(halves, shard.shape[0] // halves, shard.shape[1]), half
    )
    up_keep, up_send = line.mark(
        split_columns(line.gate(numbers(core, half)), up_weight, columns, 0, "split_up")
    )

    gathered_vec = jnp.zeros((columns,) + vectors.shape, BF16)
    gathered_vec = place(gathered_vec, vectors, column)
    for k in steps:
        gathered_vec = place(gathered_vec, vec_x[k - 1], (column - k) % columns)
    gathered_vec = line.mark(line.gate(gathered_vec))
    vec_core = over_core(gathered_vec)
    out_part = line.mark(own_half(line.gate(out_weight)))
    out_x = [over_x(out_part, k) for k in steps]

    own_image = line.pass_on(jnp.where(half == core, own_tokens, other_tokens))
    other_image = over_core(own_image)
    up_core = over_core(line.pass_on(up_send))

    mine_vec = gathered_vec.reshape(columns, -1).astype(F32)
    all_vec = by_core(gathered_vec, vec_core, 1).reshape(columns * 2, -1)
    all_vec = all_vec.astype(F32)
    vec = lambda i: all_vec[:, i * owned : (i + 1) * owned].reshape(1, width)
    own_vec = lambda i: mine_vec[:, i * owned : (i + 1) * owned].reshape(1, width // 2)
    gain_one, shift_one, gain_two, shift_two = vec(3), vec(4), vec(5), vec(6)
    vec_out, vec_down = vec(2), vec(7)
    vec_up = mine_vec[:, 8 * owned :].reshape(1, columns * owned_hidden)
    vec_qkv = jnp.concatenate(
        [own_vec(0), jnp.zeros((1, width // 2), F32), own_vec(1)], axis=1
    )
    image, first_low = line.mark(
        norm_one(line.gate(numbers(core)), own_image, other_image, gain_one, shift_one)
    )
    eighth = owned // halves // 2
    up_part = line.mark(pair_part(line.gate(numbers(core, quarter)), up_keep, up_core, eighth))
    up_x = [over_x(up_part, k) for k in steps]

    source = lambda k: (column - k) % columns
    qkv_pieces = [
        (qkv_keep, 0, owned, member),
        (qkv_core, 0, owned, member + 1 - 2 * core),
    ]
    part = owned // halves
    for k in steps:
        for value, c in ((qkv_x[k - 1][0], core), (qkv_x[k - 1][1], 1 - core)):
            value = line.pass_on(value)
            at = (2 * source(k) + c) * halves
            qkv_pieces += [(value, 0, part, at + half), (over_y(value), 0, part, at + other_half)]
    own_cotangent = line.mark(
        jnp.concatenate([line.gate(cotangent[0]), jnp.zeros((padded - rows, width), BF16)], axis=0)
    )
    other_cotangent = swap(own_cotangent)
    out_pieces = [(out_weight, 0, owned, column)]
    for k in steps:
        value = line.pass_on(out_x[k - 1])
        at = source(k) * halves
        out_pieces += [(value, 0, part, at + half), (over_y(value), 0, part, at + other_half)]
    down_part = line.mark(own_half(line.gate(down_weight)))
    down_x = [over_x(down_part, k) for k in steps]
    up_pieces = [(up_keep, 0, owned, member), (up_core, 0, owned, member + 1 - 2 * core)]

    def up_rows(value, k, h, s):
        for c in range(2):
            at = (2 * source(k) + c) * halves * 2 + h * 2 + s
            up_pieces.append((value, c * eighth, eighth, at))

    up_y = []
    for k in steps:
        value = line.pass_on(up_x[k - 1])
        up_rows(value, k, half, side)
        up_rows(over_z(value, 1), k, half, 1 - side)
        up_y.append(over_y(value))

    wqkv, qkv = join_dot(
        line, first_low, qkv_pieces, vec_qkv, lambda total: (total,), 1, width // 2, "project"
    )
    mixed, log_total = line.mark(attention(line.gate(numbers(core)), image, qkv, rows))
    for k in steps:
        value = line.pass_on(up_y[k - 1])
        up_rows(value, k, other_half, side)
        up_rows(over_z(value, 1), k, other_half, 1 - side)
    no_bias = jnp.zeros((1, width), F32)
    wout, branch = join_dot(
        line, mixed, out_pieces, no_bias, lambda total: (total,), 1, width // 2, "project_out"
    )
    branch_other = over_core(branch)
    middle, second_low = line.mark(
        norm_two(
            line.gate(numbers(core)), image, branch, branch_other, vec_out, gain_two, shift_two
        )
    )
    down_others = []
    for k in steps:
        value = line.pass_on(down_x[k - 1])
        down_others += [(value, source(k) * halves + half), (over_y(value), source(k) * halves + other_half)]
    wup, act_low, slope = join_dot(line, second_low, up_pieces, vec_up, activate, 2, 512, "hidden")
    own_incoming = line.pass_on(jnp.where(half == core, own_cotangent, other_cotangent))
    incoming = by_core(own_incoming, over_core(own_incoming)).reshape(2 * padded, width)

    class Total:
        def __init__(self, quadrant, lead, cross):
            self.quadrant, self.lead, self.cross = quadrant, lead, cross

        def along_x(self, y):
            sent = [self.quadrant((column + k) % columns, y, ()) for k in steps]
            return tuple(over_x(v, k) for k, v in zip(steps, sent))

        def first(self):
            self.got = self.along_x(other_half)

        def second(self):
            self.got_b = self.along_x(half)

        def third(self):
            self.from_y = over_y(self.quadrant(column, other_half, self.got))

        def fourth(self):
            total = self.quadrant(column, half, self.got_b + (self.from_y,))
            height = total.shape[0] // self.lead // replicas
            self.total = total.reshape(self.lead, replicas, height, total.shape[1])
            self.got_z = [over_z(pick(self.total, copy_id ^ s, 1), s) for s in range(1, replicas)]

        def fifth(self):
            total = line.gate(pick(self.total, copy_id, 1)).astype(F32)
            for value in self.got_z:
                total = total + value.astype(F32)
            total = line.mark(total.astype(BF16))
            return self.cross(total) if self.cross else total[0]

    def collect(total):
        return lax.all_gather(total, ("seq", "rep"), axis=0, tiled=False)

    def cross_cores(blocks):
        def exchange(total):
            got = over_core(pick(total, 1 - core))
            own = pick(total, core)
            one = own.shape[1] // blocks
            left = jnp.where(core == 0, own, got)
            right = jnp.where(core == 0, got, own)
            cols = []
            for k in range(blocks):
                cols += [left[:, k * one : (k + 1) * one], right[:, k * one : (k + 1) * one]]
            return cols

        return exchange

    def by_row(left, right):
        height = owned // halves

        def quadrant(x, y, added):
            blocks = numbers(*[(x * 2 + i) * halves + y for i in range(2)])
            return line.mark(weight_grad(left, right, line.gate(blocks), height, added))

        return quadrant

    def down_quadrant(x, y, added):
        blocks = line.gate(numbers(x * halves + y))
        return line.mark(weight_grad(act_low, incoming, blocks, owned_hidden // halves, added))

    def out_quadrant(x, y, added):
        at = line.gate(numbers(x * halves + y, x, y))
        return line.mark(
            out_grad(at, mixed, branch_low, vec_grads, owned // halves, replicas, added)
        )

    pieces = halves * replicas
    total_down = Total(down_quadrant, 1, None)
    total_down.first()
    total_down.second()

    at = [column * halves + h for h in range(halves)] + [place_ for _, place_ in down_others]
    hidden_low, up_sums, partial = line.mark(
        feed_back(
            line.gate(numbers(*at)),
            incoming,
            act_low,
            slope,
            down_weight,
            [value for value, _ in down_others],
        )
    )
    total_up = Total(by_row(second_low, hidden_low), 2, cross_cores(columns))
    grad_second = line.mark(
        dot_rows(line.gate(numbers(core)), hidden_low, wup, width // 2, "grad_second")
    )
    grad_second_other = over_core(grad_second)
    total_up.first()
    total_up.second()
    grad_middle, branch_low, sums_two = line.mark(
        norm_two_back(
            line.gate(numbers(core)), incoming, grad_second, grad_second_other, middle, gain_two
        )
    )
    grad_mixed = line.mark(
        dot_rows(line.gate(numbers(core)), branch_low, wout, width // 2, "grad_mixed")
    )
    total_down.third()
    grad_qkv, qv_sums = line.mark(
        attention_grad(line.gate(numbers(core)), image, qkv, grad_mixed, log_total, rows)
    )
    grad_first = line.mark(
        dot_rows(line.gate(numbers(core)), grad_qkv, wqkv, width // 2, "grad_first")
    )
    grad_first_other = over_core(grad_first)
    total_qkv = Total(by_row(first_low, grad_qkv), 2, cross_cores(3 * columns))
    total_qkv.first()
    total_qkv.second()
    total_down.fourth()
    own_grad, own_grad_low, sums_one = line.mark(
        norm_one_back(
            line.gate(numbers(core)), grad_middle, grad_first, grad_first_other, image, gain_one
        )
    )

    entries = 8 * owned + owned_hidden
    vec_grads = line.mark(
        run(
            functools.partial(pack_body, columns, owned, replicas, entries // pieces),
            "pack_vectors",
            (1,),
            line.gate(numbers(core)),
            (sums_two, sums_one, qv_sums, up_sums),
            [
                whole(8, width),
                whole(8, width),
                whole(*qv_sums.shape),
                whole(*up_sums.shape),
            ],
            [((columns, 8 * pieces, width), F32, whole(columns, 8 * pieces, width))],
        )[0]
    )
    total_out = Total(out_quadrant, 1, None)
    total_out.first()
    total_out.second()
    total_up.third()

    halves_of = lambda value: value.reshape(2, padded, width)
    from_other = over_core(line.pass_on(pick(halves_of(partial), 1 - core)))
    grad_down = collect(total_down.fifth())
    block = pick(halves_of(middle), core) + pick(halves_of(partial), core).astype(F32)
    block = line.mark((line.gate(block) + from_other.astype(F32) + vec_down).astype(BF16))
    block_moved = swap(block)
    moved = swap(line.pass_on(own_grad_low))
    total_up.fourth()
    total_qkv.third()
    up_cols = total_up.fifth()
    grad_up = collect(jnp.concatenate(up_cols, axis=1))
    total_qkv.fourth()
    total_out.third()
    block_out = line.mark(jnp.where(half == core, line.gate(block), block_moved)[:rows][None])
    token_grad = line.mark(
        jnp.where(half == core, line.gate(own_grad), moved.astype(F32))[:rows][None]
    )
    total_out.fourth()
    qkv_cols = total_qkv.fifth()
    out_rows = total_out.fifth()
    height = out_rows.shape[0] - 8
    each = 2 * columns
    joined = [jnp.concatenate(qkv_cols[each * p : each * p + each], axis=1) for p in range(3)]
    joined = collect(jnp.concatenate(joined + [out_rows], axis=0))
    grad_down = line.mark(line.gate(grad_down).astype(F32).reshape(owned_hidden, width))
    grad_up = line.mark(line.gate(grad_up).astype(F32).reshape(owned, up_weight.shape[1]))
    joined = line.gate(joined).reshape(pieces, -1, width)
    grad_qkv_w = jnp.concatenate(
        [joined[:, p * height : (p + 1) * height] for p in range(3)], axis=2
    )
    grad_qkv_w = grad_qkv_w.astype(F32).reshape(owned, 3 * width)
    grad_out = joined[:, 3 * height : 4 * height].astype(F32).reshape(owned, width)
    vec_out_grads = joined[:, 4 * height, : entries // pieces].astype(F32).reshape(entries)
    vec_of = lambda i: vec_out_grads[i * owned : (i + 1) * owned]
    return (
        block_out,
        token_grad,
        grad_qkv_w,
        vec_of(0),
        vec_of(1),
        grad_out,
        vec_of(2),
        vec_of(3),
        vec_of(4),
        vec_of(5),
        vec_of(6),
        grad_up,
        vec_out_grads[8 * owned :],
        grad_down,
        vec_of(7),
    )


def solution(mesh):
    return jax.shard_map(
        shards,
        mesh=mesh,
        in_specs=(
            P(("shard", "rep"), "seq", None),
            P(("shard", "rep")),
            P("shard", None),
            P("shard"),
            P("shard"),
            P("shard", None),
            P("shard"),
            P("shard"),
            P("shard"),
            P("shard"),
            P("shard"),
            P("shard", None),
            P("shard"),
            P("shard", None),
            P("shard"),
            P(("shard", "rep"), "seq", None),
        ),
        out_specs=(
            P(("shard", "rep"), "seq", None),
            P(("shard", "rep"), "seq", None),
            P("shard", None),
            P("shard"),
            P("shard"),
            P("shard", None),
            P("shard"),
            P("shard"),
            P("shard"),
            P("shard"),
            P("shard"),
            P("shard", None),
            P("shard"),
            P("shard", None),
            P("shard"),
        ),
        check_vma=False,
    )
```

```python
import functools
import math

import jax
import jax.numpy as jnp
from jax import lax
from jax.experimental import pallas as pl
from jax.experimental.pallas import tpu as pltpu
from jax.sharding import PartitionSpec as P

H = 16
HD = 64
EPS = 1e-06
F32 = jnp.float32
BF16 = jnp.bfloat16
VMEM_LIMIT = 48 * 1024 * 1024
HINT = pl.CostEstimate(flops=200_000_000_000, transcendentals=0, bytes_accessed=20_000_000)


def dims(left, right, dot_left, dot_right):
    return lax.dot_general(
        left, right, (((dot_left,), (dot_right,)), ((), ())), preferred_element_type=F32
    )


def whole(*shape):
    return pl.BlockSpec(shape, lambda *index: (0,) * len(shape))


def run(body, name, grid, place, operands, in_specs, outs, scratch=()):
    return pl.pallas_call(
        body,
        grid_spec=pltpu.PrefetchScalarGridSpec(
            num_scalar_prefetch=1,
            grid=grid,
            in_specs=in_specs,
            out_specs=[out[2] for out in outs],
            scratch_shapes=list(scratch),
        ),
        out_shape=[jax.ShapeDtypeStruct(out[0], out[1]) for out in outs],
        compiler_params=pltpu.CompilerParams(vmem_limit_bytes=VMEM_LIMIT),
        cost_estimate=HINT,
        name=name,
    )(place, *operands)


def numbers(*values):
    return jnp.stack([jnp.asarray(value, jnp.int32) for value in values])


def key_visible(note_ref, padded_half, rows):
    note = note_ref[...].astype(F32)[rows % 16 : rows % 16 + 1, :]
    length = note[:, 0:1] * 16.0 + note[:, 1:2]
    row = lax.broadcasted_iota(jnp.int32, (2 * padded_half, 1), 0)
    second = row >= padded_half
    inside = jnp.where(second, row - padded_half, row)
    position = jnp.where(second, inside + rows, inside)
    return (inside < rows) & (position.astype(F32) < length)


def attend_forward(padded_half, rows, place_ref, note_ref, q_ref, k_ref, v_ref, mixed_ref, log_ref):
    visible = key_visible(note_ref, padded_half, rows)
    for head in range(2):
        lanes = slice(head * HD, (head + 1) * HD)
        scores = dims(k_ref[:, lanes], q_ref[:, lanes], 1, 1) * (HD ** -0.5)
        scores = jnp.where(visible, scores, -1000000000.0)
        top = jnp.max(scores, axis=0, keepdims=True)
        shifted = jnp.exp(scores - top)
        total = jnp.sum(shifted, axis=0, keepdims=True)
        weights = (shifted * (1.0 / total)).astype(BF16)
        log_ref[0, head : head + 1, :] = top + jnp.log(total)
        values = jnp.transpose(v_ref[:, lanes].astype(F32)).astype(BF16)
        mixed = dims(values, weights, 1, 0)
        mixed_ref[:, lanes] = jnp.transpose(mixed).astype(BF16)


def attend_backward(
    padded_half, rows, place_ref, note_ref, q_ref, k_ref, v_ref, g_ref, log_ref, out_ref, sum_ref
):
    visible = key_visible(note_ref, padded_half, rows)
    for head in range(2):
        lanes = slice(head * HD, (head + 1) * HD)
        queries, keys = q_ref[:, lanes], k_ref[:, lanes]
        values, grads = v_ref[:, lanes], g_ref[:, lanes]
        scores = dims(keys, queries, 1, 1) * (HD ** -0.5)
        weights = jnp.where(visible, jnp.exp(scores - log_ref[0, head : head + 1, :]), 0.0)
        grad_weights = dims(values, grads, 1, 1)
        inner = jnp.sum(weights * grad_weights, axis=0, keepdims=True)
        grad_scores = (weights * (grad_weights - inner)).astype(BF16)
        keys_t = jnp.transpose(keys.astype(F32)).astype(BF16)
        grad_q = (jnp.transpose(dims(keys_t, grad_scores, 1, 0)) * (HD ** -0.5)).astype(BF16)
        grad_v = dims(weights.astype(BF16), grads, 1, 0).astype(BF16)
        out_ref[0, :, lanes] = grad_q
        out_ref[1, :, lanes] = (dims(grad_scores, queries, 1, 0) * (HD ** -0.5)).astype(BF16)
        out_ref[2, :, lanes] = grad_v
        sum_ref[0, 0:1, lanes] = jnp.sum(grad_q.astype(F32), axis=0, keepdims=True)
        sum_ref[0, 1:2, lanes] = jnp.sum(grad_v.astype(F32), axis=0, keepdims=True)


def attention(place, image, qkv, rows):
    tokens, width = qkv.shape
    pairs = width // 3 // (2 * HD)
    part = lambda p: pl.BlockSpec((tokens, 2 * HD), lambda j, n, p=p: (0, p * pairs + j))
    return run(
        functools.partial(attend_forward, tokens // 2, rows),
        "attention",
        (pairs,),
        place,
        (image, qkv, qkv, qkv),
        [pl.BlockSpec((16, 128), lambda j, n: (rows // 16, 0)), part(0), part(1), part(2)],
        [
            ((tokens, width // 3), BF16, pl.BlockSpec((tokens, 2 * HD), lambda j, n: (0, j))),
            ((pairs, 2, tokens), F32, pl.BlockSpec((1, 2, tokens), lambda j, n: (j, 0, 0))),
        ],
    )


def attention_grad(place, image, qkv, grad_mixed, log_total, rows):
    tokens, width = qkv.shape
    pairs = width // 3 // (2 * HD)
    part = lambda p: pl.BlockSpec((tokens, 2 * HD), lambda j, n, p=p: (0, p * pairs + j))
    return run(
        functools.partial(attend_backward, tokens // 2, rows),
        "attention_grad",
        (pairs,),
        place,
        (image, qkv, qkv, qkv, grad_mixed, log_total),
        [
            pl.BlockSpec((16, 128), lambda j, n: (rows // 16, 0)),
            part(0),
            part(1),
            part(2),
            pl.BlockSpec((tokens, 2 * HD), lambda j, n: (0, j)),
            pl.BlockSpec((1, 2, tokens), lambda j, n: (j, 0, 0)),
        ],
        [
            (
                (3, tokens, width // 3),
                BF16,
                pl.BlockSpec((3, tokens, 2 * HD), lambda j, n: (0, 0, j)),
            ),
            ((pairs, 8, 2 * HD), F32, pl.BlockSpec((1, 8, 2 * HD), lambda j, n: (j, 0, 0))),
        ],
    )


def norm_one_body(place_ref, own_ref, other_ref, gain_ref, shift_ref, image_ref, low_ref):
    def write(values_ref):
        normal, _ = normalize(values_ref[...].astype(F32))
        image_ref[...] = values_ref[...]
        low_ref[...] = (normal * gain_ref[...] + shift_ref[...]).astype(BF16)

    mine = pl.program_id(0) == place_ref[0]
    pl.when(mine)(lambda: write(own_ref))
    pl.when(jnp.logical_not(mine))(lambda: write(other_ref))


def norm_one(place, own, other, gain, shift):
    padded, width = own.shape
    rows = pl.BlockSpec((padded, width), lambda i, n: (i, 0))
    shape = (2 * padded, width)
    return run(
        norm_one_body,
        "norm_one",
        (2,),
        place,
        (own, other, gain, shift),
        [whole(padded, width)] * 2 + [whole(1, width)] * 2,
        [(shape, BF16, rows)] * 2,
    )


def norm_two_body(
    place_ref, image_ref, own_ref, other_ref, bias_ref, gain_ref, shift_ref, middle_ref, low_ref
):
    branch = own_ref[...].astype(F32) + other_ref[...].astype(F32)
    middle = image_ref[...].astype(F32) + branch + bias_ref[...]
    normal, _ = normalize(middle)
    middle_ref[...] = middle
    low_ref[...] = (normal * gain_ref[...] + shift_ref[...]).astype(BF16)


def norm_two(place, image, own, other, bias, gain, shift):
    tokens, width = image.shape
    rows = pl.BlockSpec((tokens // 2, width), lambda i, n: (i, 0))
    return run(
        norm_two_body,
        "norm_two",
        (2,),
        place,
        (image, own, other, bias, gain, shift),
        [rows] * 3 + [whole(1, width)] * 3,
        [((tokens, width), F32, rows), ((tokens, width), BF16, rows)],
    )


def add_sums(sum_ref, values):
    @pl.when(pl.program_id(0) == 0)
    def _():
        sum_ref[...] = jnp.zeros_like(sum_ref)

    for k, value in enumerate(values):
        sum_ref[k : k + 1, :] += jnp.sum(value, axis=0, keepdims=True)


def norm_two_back_body(
    place_ref, incoming_ref, own_ref, other_ref, middle_ref, gain_ref, grad_ref, low_ref, sum_ref
):
    incoming = incoming_ref[...].astype(F32)
    grad = own_ref[...].astype(F32) + other_ref[...].astype(F32)
    normal, scale = normalize(middle_ref[...])
    grad_middle = incoming + normalize_grad(grad, gain_ref[...], normal, scale)
    low = grad_middle.astype(BF16)
    grad_ref[...] = grad_middle
    low_ref[...] = low
    add_sums(sum_ref, (grad * normal, grad, low.astype(F32), incoming))


def norm_two_back(place, incoming, own, other, middle, gain):
    tokens, width = incoming.shape
    rows = pl.BlockSpec((tokens // 2, width), lambda i, n: (i, 0))
    return run(
        norm_two_back_body,
        "norm_two_back",
        (2,),
        place,
        (incoming, own, other, middle, gain),
        [rows] * 4 + [whole(1, width)],
        [((tokens, width), F32, rows), ((tokens, width), BF16, rows), ((8, width), F32, whole(8, width))],
    )


def norm_one_back_body(
    place_ref, grad_ref, own_ref, other_ref, image_ref, gain_ref, kept_ref, low_ref, sum_ref
):
    grad = own_ref[...].astype(F32) + other_ref[...].astype(F32)
    normal, scale = normalize(image_ref[...].astype(F32))
    total = grad_ref[...] + normalize_grad(grad, gain_ref[...], normal, scale)
    add_sums(sum_ref, (grad * normal, grad))

    @pl.when(pl.program_id(0) == place_ref[0])
    def _():
        kept_ref[...] = total
        low_ref[...] = total.astype(BF16)


def norm_one_back(place, grad_middle, own, other, image, gain):
    tokens, width = image.shape
    padded = tokens // 2
    rows = pl.BlockSpec((padded, width), lambda i, n: (i, 0))
    return run(
        norm_one_back_body,
        "norm_one_back",
        (2,),
        place,
        (grad_middle, own, other, image, gain),
        [rows] * 4 + [whole(1, width)],
        [
            ((padded, width), F32, whole(padded, width)),
            ((padded, width), BF16, whole(padded, width)),
            ((8, width), F32, whole(8, width)),
        ],
    )


def split_body(part_rows, place_ref, keep_in, send_in, keep, send, *parts):
    keep[...] = keep_in[...]
    send[...] = send_in[...]
    if parts:
        first = pl.multiple_of(place_ref[1] * part_rows, part_rows)
        parts[0][...] = keep_in[pl.ds(first, part_rows), :]
        parts[1][...] = send_in[pl.ds(first, part_rows), :]


def split_columns(place, shard, number, part_rows, name):
    depth, wide = shard.shape
    one = wide // number // 2
    out = lambda rows: ((rows, wide // 2), BF16, pl.BlockSpec((rows, one), lambda j, n: (0, j)))
    return run(
        functools.partial(split_body, part_rows),
        name,
        (number,),
        place,
        (shard, shard),
        [
            pl.BlockSpec((depth, one), lambda j, n: (0, 2 * j + n[0])),
            pl.BlockSpec((depth, one), lambda j, n: (0, 2 * j + 1 - n[0])),
        ],
        [out(depth)] * 2 + ([out(part_rows)] * 2 if part_rows else []),
    )


def pair_body(rows, place_ref, own_ref, other_ref, out_ref):
    first = pl.multiple_of(place_ref[1] * rows, rows)
    zero = place_ref[0] == 0
    own, other = own_ref[pl.ds(first, rows), :], other_ref[pl.ds(first, rows), :]
    out_ref[:rows, :] = jnp.where(zero, own, other)
    out_ref[rows:, :] = jnp.where(zero, other, own)


def pair_part(place, own, other, rows):
    depth, wide = own.shape
    tile = wide // 2
    return run(
        functools.partial(pair_body, rows),
        "pair_part",
        (2,),
        place,
        (own, other),
        [pl.BlockSpec((depth, tile), lambda j, n: (0, j))] * 2,
        [((2 * rows, wide), BF16, pl.BlockSpec((2 * rows, tile), lambda j, n: (0, j)))],
    )[0]


def join_body(blocks, count, finish, place_ref, left_ref, bias_ref, *refs):
    pieces, joined_ref, outs = refs[:count], refs[count], refs[count + 1 :]
    for k, (number, source, rows) in enumerate(blocks):
        first = pl.multiple_of(place_ref[k] * rows, rows)
        joined_ref[pl.ds(first, rows), :] = pieces[number][source : source + rows, :]
    total = dims(left_ref[...], joined_ref[...], 1, 0) + bias_ref[...]
    for out, value in zip(outs, finish(total)):
        out[...] = value.astype(out.dtype)


def join_dot(line, left, pieces, bias, finish, results, tile, name):
    arrays = []
    for piece in pieces:
        if not any(piece[0] is array for array in arrays):
            arrays.append(piece[0])
    number = lambda array: [array is other for other in arrays].index(True)
    blocks = [(number(array), source, rows) for array, source, rows, _ in pieces]
    place = line.gate(numbers(*[piece[3] for piece in pieces]))
    tokens, depth = left.shape
    wide = arrays[0].shape[1]
    spec = lambda rows: pl.BlockSpec((rows, tile), lambda j, n: (0, j))
    return line.mark(
        run(
            functools.partial(join_body, blocks, len(arrays), finish),
            name,
            (wide // tile,),
            place,
            (left, bias) + tuple(arrays),
            [whole(tokens, depth), spec(1)] + [spec(array.shape[0]) for array in arrays],
            [((depth, wide), BF16, spec(depth))] + [((tokens, wide), BF16, spec(tokens))] * results,
        )
    )


def activate(hidden):
    normal = 0.5 * (1.0 + lax.erf(hidden * math.sqrt(0.5)))
    density = jnp.exp(-0.5 * hidden * hidden) * (1.0 / math.sqrt(2.0 * math.pi))
    return hidden * normal, normal + hidden * density


def feed_back_body(
    own_blocks, count, place_ref, incoming_ref, act_ref, slope_ref, own_ref, *refs
):
    others, (low_ref, sum_ref, part_ref), (weight_ref, total_ref) = (
        refs[:count],
        refs[count : count + 3],
        refs[count + 3 :],
    )
    step = pl.program_id(0)

    @pl.when(step < own_blocks)
    def _():
        weight_ref[...] = own_ref[...]

    for k in range(count):

        @pl.when(step == own_blocks + k)
        def _(k=k):
            weight_ref[...] = others[k][...]

    grad = dims(incoming_ref[...], weight_ref[...], 1, 1) * slope_ref[...].astype(F32)
    low = grad.astype(BF16)
    low_ref[...] = low
    sum_ref[...] = jnp.sum(low.astype(F32), axis=0, keepdims=True)
    part = dims(act_ref[...], weight_ref[...], 1, 0)
    total = jnp.where(step == 0, part, total_ref[...] + part)
    total_ref[...] = total

    @pl.when(step == own_blocks + count - 1)
    def _():
        part_ref[...] = total.astype(BF16)


def feed_back(place, incoming, act, slope, own, others):
    tokens, width = incoming.shape
    hidden = act.shape[1]
    tile = others[0].shape[0]
    own_blocks = own.shape[0] // tile
    steps = own_blocks + len(others)
    block = pl.BlockSpec((tokens, tile), lambda s, n: (0, n[s]))
    return run(
        functools.partial(feed_back_body, own_blocks, len(others)),
        "feed_back",
        (steps,),
        place,
        (incoming, act, slope, own) + tuple(others),
        [
            whole(tokens, width),
            block,
            block,
            pl.BlockSpec((tile, width), lambda s, n: (jnp.minimum(s, own_blocks - 1), 0)),
        ]
        + [whole(tile, width)] * len(others),
        [
            ((tokens, hidden), BF16, block),
            ((1, hidden), F32, pl.BlockSpec((1, tile), lambda s, n: (0, n[s]))),
            ((tokens, width), BF16, whole(tokens, width)),
        ],
        [pltpu.VMEM((tile, width), BF16), pltpu.VMEM((tokens, width), F32)],
    )


def dot_rows_body(place_ref, left_ref, weight_ref, out_ref):
    parts = left_ref.shape[0] if len(left_ref.shape) == 3 else 1
    if parts == 1:
        total = dims(left_ref[...], weight_ref[...], 1, 1)
    else:
        one = left_ref.shape[2]
        total = dims(left_ref[0], weight_ref[:, :one], 1, 1)
        for p in range(1, parts):
            total = total + dims(left_ref[p], weight_ref[:, p * one : (p + 1) * one], 1, 1)
    out_ref[...] = total.astype(BF16)


def dot_rows(place, left, weight, tile, name):
    tokens = left.shape[-2]
    rows, depth = weight.shape
    return run(
        dot_rows_body,
        name,
        (rows // tile,),
        place,
        (left, weight),
        [whole(*left.shape), pl.BlockSpec((tile, depth), lambda j, n: (j, 0))],
        [((tokens, rows), BF16, pl.BlockSpec((tokens, tile), lambda j, n: (0, j)))],
    )[0]


def pack_body(columns, owned, replicas, share, place_ref, two_ref, one_ref, qv_ref, up_ref, out_ref):
    zero = place_ref[0] == 0
    pairs = qv_ref.shape[0] // columns
    hidden = up_ref.shape[1] // columns
    out_ref[...] = jnp.zeros_like(out_ref)
    for x in range(columns):
        parts = [qv_ref[x * pairs + p, row : row + 1, :] for row in range(2) for p in range(pairs)]
        for ref, row in ((two_ref, 2), (one_ref, 0), (one_ref, 1), (two_ref, 0), (two_ref, 1), (two_ref, 3)):
            first, second = (
                ref[row : row + 1, (2 * x + c) * owned : (2 * x + c + 1) * owned] for c in range(2)
            )
            parts.append(jnp.where(zero, first, second))
        parts.append(up_ref[:, x * hidden : (x + 1) * hidden])
        row = jnp.concatenate(parts, axis=1)
        for p in range(out_ref.shape[1] // 8):
            out_ref[x, 8 * p : 8 * p + 1, :share] = row[:, p * share : (p + 1) * share]


def out_grad_body(count, replicas, place_ref, left_ref, right_ref, vec_ref, *rest):
    total = dims(left_ref[...], right_ref[...], 0, 0)
    height = total.shape[0] // replicas
    every = height + 8
    for z in range(replicas):
        for first, value in (
            (z * every, total[z * height : (z + 1) * height]),
            (z * every + height, vec_ref[0, 8 * z : 8 * z + 8, :]),
        ):
            rows = slice(first, first + value.shape[0])
            for added in rest[:count]:
                value = value + added[rows, :].astype(F32)
            rest[count][rows, :] = value.astype(BF16)


def out_grad(place, left, right, vectors, height, replicas, added=()):
    tokens, width = right.shape
    every = height + 8 * replicas
    if height % 128:
        left = lax.dynamic_slice_in_dim(left, place[0] * height, height, 1)
        place = place * numbers(0, 1, 1)
    return run(
        functools.partial(out_grad_body, len(added), replicas),
        "out_grad",
        (1,),
        place,
        (left, right, vectors) + tuple(added),
        [
            pl.BlockSpec((tokens, height), lambda i, n: (0, n[0])),
            whole(tokens, width),
            pl.BlockSpec((1, 8 * replicas, width), lambda i, n: (n[1], n[2], 0)),
        ]
        + [whole(every, width)] * len(added),
        [((every, width), BF16, whole(every, width))],
    )[0]


def weight_grad_body(count, index_ref, left_ref, right_ref, *rest):
    total = dims(left_ref[...], right_ref[...], 0, 0)
    for added in rest[:count]:
        total = total + added[...].astype(F32)
    rest[count][...] = total.astype(BF16)


def weight_grad(left, right, blocks, height, added=()):
    tokens = left.shape[0]
    number = blocks.shape[0]
    if height % 128:
        narrow = [
            lax.dynamic_slice_in_dim(left, blocks[i] * height, height, 1) for i in range(number)
        ]
        left = jnp.concatenate(narrow, axis=1)
        blocks = jnp.zeros((1,), jnp.int32)
        number, height = 1, number * height
    parts = right.shape[0] if right.ndim == 3 else 1
    width = right.shape[-1]
    if right.ndim == 3:
        right_spec = pl.BlockSpec((pl.Squeezed(), tokens, width), lambda i, j, n: (j, 0, 0))
    else:
        parts = 2
        width = width // parts
        right_spec = pl.BlockSpec((tokens, width), lambda i, j, n: (0, j))
    tile = pl.BlockSpec((height, width), lambda i, j, n: (i, j))
    return pl.pallas_call(
        functools.partial(weight_grad_body, len(added)),
        grid_spec=pltpu.PrefetchScalarGridSpec(
            num_scalar_prefetch=1,
            grid=(number, parts),
            in_specs=[pl.BlockSpec((tokens, height), lambda i, j, n: (0, n[i])), right_spec]
            + [tile] * len(added),
            out_specs=tile,
        ),
        out_shape=jax.ShapeDtypeStruct((number * height, parts * width), BF16),
        compiler_params=pltpu.CompilerParams(vmem_limit_bytes=VMEM_LIMIT),
        cost_estimate=HINT,
        name="weight_grad",
    )(blocks, left, right, *added)


def tick_body(place_ref, out_ref):
    out_ref[...] = jnp.full(out_ref.shape, place_ref[0], jnp.int32)


class Line:
    def __init__(self):
        self.last = None

    def gate(self, value):
        if self.last is None:
            return value
        return lax.optimization_barrier((value, self.last))[0]

    def mark(self, value):
        self.last = value
        return value

    def tick(self):
        place = self.gate(jnp.zeros((1,), jnp.int32))
        self.last = run(
            tick_body, "tick", (1,), place, (), [], [((8, 128), jnp.int32, whole(8, 128))]
        )[0]

    def pass_on(self, value):
        self.tick()
        return self.mark(self.gate(value))


def normalize(values):
    centered = values - jnp.mean(values, -1, keepdims=True)
    scale = lax.rsqrt(jnp.mean(centered * centered, -1, keepdims=True) + EPS)
    return centered * scale, scale


def normalize_grad(grad, gain, normal, scale):
    scaled = grad * gain
    return scale * (
        scaled
        - jnp.mean(scaled, -1, keepdims=True)
        - normal * jnp.mean(scaled * normal, -1, keepdims=True)
    )


def place(buffer, piece, position):
    start = (position,) + (0,) * (buffer.ndim - 1)
    return lax.dynamic_update_slice(buffer, piece[None], start)


def pick(array, index, axis=0):
    return lax.dynamic_index_in_dim(array, index, axis, keepdims=False)


def shards(
    tokens,
    lengths,
    qkv_weight,
    query_bias,
    value_bias,
    out_weight,
    out_bias,
    first_gain,
    first_shift,
    second_gain,
    second_shift,
    up_weight,
    up_bias,
    down_weight,
    down_bias,
    cotangent,
):
    _, rows, width = tokens.shape
    halves = lax.axis_size("seq")
    group = lax.axis_size("shard")
    replicas = lax.axis_size("rep")
    columns = group // 2
    half, member, copy_id = (lax.axis_index(name) for name in ("seq", "shard", "rep"))
    core, column = member % 2, member // 2
    owned = width // group
    owned_hidden = up_bias.shape[0]
    padded = -(-(rows + 1) // 16) * 16

    def over_core(value):
        return lax.ppermute(value, "shard", [(i, i ^ 1) for i in range(group)])

    def over_x(value, step):
        return lax.ppermute(value, "shard", [(i, (i + 2 * step) % group) for i in range(group)])

    def over_x_core(value, step):
        pairs = [(i, ((i + 2 * step) % group) ^ 1) for i in range(group)]
        return lax.ppermute(value, "shard", pairs)

    def over_y(value):
        return lax.ppermute(value, "seq", [(i, halves - 1 - i) for i in range(halves)])

    def over_z(value, step):
        return lax.ppermute(value, "rep", [(i, i ^ step) for i in range(replicas)])

    swaps = []
    for s in range(halves):
        for h in range(group):
            if s != h % 2:
                swaps.append((s * group + h, (h % 2) * group + (h // 2) * 2 + s))

    def swap(value):
        return lax.ppermute(value, ("seq", "shard"), swaps)

    def by_core(mine, other, axis=0):
        return jnp.where(
            core == 0, jnp.stack([mine, other], axis), jnp.stack([other, mine], axis)
        )

    line = Line()
    steps = range(1, columns)
    other_half = halves - 1 - half
    side = copy_id % 2
    quarter = half * 2 + side

    length = lengths[0]
    lane = lax.broadcasted_iota(jnp.int32, (padded - rows, width), 1)
    note = jnp.where(lane == 0, length // 16, jnp.where(lane == 1, length % 16, 0)).astype(BF16)
    own_tokens = line.mark(jnp.concatenate([tokens[0], note], axis=0))
    other_tokens = swap(own_tokens)

    qkv_keep, qkv_send, qkv_part, qkv_cross = line.mark(
        split_columns(
            line.gate(numbers(core, half)), qkv_weight, 3 * columns, owned // halves, "split_qkv"
        )
    )
    qkv_x = [(over_x(qkv_part, k), over_x_core(qkv_cross, k)) for k in steps]

    singles = [
        query_bias,
        value_bias,
        out_bias,
        first_gain,
        first_shift,
        second_gain,
        second_shift,
        down_bias,
    ]
    singles += [up_bias[i * owned : (i + 1) * owned] for i in range(owned_hidden // owned)]
    row_of = lax.broadcasted_iota(jnp.int32, (16, owned), 0)
    vectors = jnp.zeros((16, owned), BF16)
    for i, single in enumerate(singles):
        vectors = jnp.where(row_of == i, jnp.broadcast_to(single[None], (16, owned)), vectors)
    vectors = line.mark(line.gate(vectors))
    vec_x = [over_x(vectors, k) for k in steps]

    own_half = lambda shard: pick(
        shard.reshape(halves, shard.shape[0] // halves, shard.shape[1]), half
    )
    up_keep, up_send = line.mark(
        split_columns(line.gate(numbers(core, half)), up_weight, columns, 0, "split_up")
    )
    qkv_core = line.pass_on(over_core(line.gate(qkv_send)))
    source = lambda k: (column - k) % columns
    qkv_pieces = [
        (qkv_keep, 0, owned, member),
        (qkv_core, 0, owned, member + 1 - 2 * core),
    ]
    part = owned // halves

    def relay_qkv(index, c):
        for k in steps:
            value = line.pass_on(qkv_x[k - 1][index])
            at = (2 * source(k) + c) * halves
            qkv_pieces.append((value, 0, part, at + half))
            qkv_pieces.append((over_y(value), 0, part, at + other_half))

    own_image = line.pass_on(jnp.where(half == core, own_tokens, line.pass_on(other_tokens)))
    other_image = line.pass_on(over_core(own_image))
    relay_qkv(0, core)
    up_core = line.pass_on(over_core(line.gate(up_send)))
    eighth = owned // halves // 2
    up_part = line.mark(pair_part(line.gate(numbers(core, quarter)), up_keep, up_core, eighth))
    out_part = line.mark(own_half(line.gate(out_weight)))
    relay_qkv(1, 1 - core)
    out_x = [over_x(line.gate(out_part), k) for k in steps]

    gathered_vec = jnp.zeros((columns,) + vectors.shape, BF16)
    gathered_vec = place(gathered_vec, vectors, column)
    for k in steps:
        gathered_vec = place(gathered_vec, line.pass_on(vec_x[k - 1]), (column - k) % columns)
    line.mark(gathered_vec)
    vec_core = line.pass_on(over_core(gathered_vec))
    up_x = [over_x(line.gate(up_part), k) for k in steps]

    mine_vec = gathered_vec.astype(F32)
    all_vec = by_core(gathered_vec, vec_core, 1).reshape(columns * 2, 16, owned)
    all_vec = all_vec.astype(F32)
    vec = lambda i: all_vec[:, i].reshape(1, width)
    own_vec = lambda i: mine_vec[:, i].reshape(1, width // 2)
    gain_one, shift_one, gain_two, shift_two = vec(3), vec(4), vec(5), vec(6)
    vec_out, vec_down = vec(2), vec(7)
    vec_up = mine_vec[:, 8 : 8 + owned_hidden // owned].reshape(1, columns * owned_hidden)
    vec_qkv = jnp.concatenate(
        [own_vec(0), jnp.zeros((1, width // 2), F32), own_vec(1)], axis=1
    )
    image, first_low = line.mark(
        norm_one(line.gate(numbers(core)), own_image, other_image, gain_one, shift_one)
    )
    own_cotangent = line.mark(
        jnp.concatenate([line.gate(cotangent[0]), jnp.zeros((padded - rows, width), BF16)], axis=0)
    )
    chunks = 2
    down_part = line.mark(
        own_half(line.gate(down_weight)).reshape(chunks, -1, width)
    )
    out_pieces = [(out_weight, 0, owned, column)]
    for k in steps:
        value = line.pass_on(out_x[k - 1])
        at = source(k) * halves
        out_pieces += [(value, 0, part, at + half), (over_y(value), 0, part, at + other_half)]
    down_x = [[over_x(line.gate(down_part[0]), k) for k in steps]]

    wqkv, qkv = join_dot(
        line, first_low, qkv_pieces, vec_qkv, lambda total: (total,), 1, width // 2, "project"
    )
    up_pieces = [(up_keep, 0, owned, member), (up_core, 0, owned, member + 1 - 2 * core)]

    def up_rows(value, k, h, s):
        for c in range(2):
            at = (2 * source(k) + c) * halves * 2 + h * 2 + s
            up_pieces.append((value, c * eighth, eighth, at))

    up_y, up_z, down_others = [], [], []
    no_bias = jnp.zeros((1, width), F32)

    def relay_down(c):
        for k in steps:
            value = line.pass_on(down_x[c][k - 1])
            at = source(k) * halves * chunks + c
            down_others.append((value, at + half * chunks))
            down_others.append((over_y(value), at + other_half * chunks))

    other_cotangent = swap(line.gate(own_cotangent))
    for k in steps:
        value = line.pass_on(up_x[k - 1])
        up_rows(value, k, half, side)
        up_z.append(over_z(value, 1))
        up_y.append(over_y(value))
    mixed, log_total = line.mark(attention(line.gate(numbers(core)), image, qkv, rows))
    wout, branch = join_dot(
        line, mixed, out_pieces, no_bias, lambda total: (total,), 1, width // 2, "project_out"
    )
    branch_other = over_core(branch)
    for k in steps:
        up_rows(line.pass_on(up_z[k - 1]), k, half, 1 - side)
    for k in steps:
        value = line.pass_on(up_y[k - 1])
        up_rows(value, k, other_half, side)
        up_y[k - 1] = over_z(value, 1)
    relay_down(0)
    line.tick()
    down_x.append([over_x(line.gate(down_part[1]), k) for k in steps])
    middle, second_low = line.mark(
        norm_two(
            line.gate(numbers(core)), image, branch, branch_other, vec_out, gain_two, shift_two
        )
    )
    other_cotangent = line.pass_on(other_cotangent)
    own_incoming = line.mark(jnp.where(half == core, own_cotangent, other_cotangent))
    incoming_other = over_core(own_incoming)
    incoming_other = line.pass_on(incoming_other)
    incoming = line.mark(by_core(own_incoming, incoming_other).reshape(2 * padded, width))
    for k in steps:
        up_rows(line.pass_on(up_y[k - 1]), k, other_half, 1 - side)
    wup, act_low, slope = join_dot(line, second_low, up_pieces, vec_up, activate, 2, 512, "hidden")

    class Total:
        def __init__(self, quadrant, lead, cross):
            self.quadrant, self.lead, self.cross = quadrant, lead, cross
            self.crossed = not cross
            self.halving, self.done, self.step = True, False, 1

        def along_x(self, y):
            return [self.quadrant((column + k) % columns, y, ()) for k in steps]

        def make_first(self):
            self.sent = self.along_x(other_half)

        def make_second(self):
            self.sent_b = self.along_x(half)

        def first(self):
            self.got = tuple(over_x(line.gate(v), k) for k, v in zip(steps, self.sent))

        def second(self):
            self.got_b = tuple(over_x(line.gate(v), k) for k, v in zip(steps, self.sent_b))

        def third(self):
            line.tick()
            self.from_y = over_y(self.quadrant(column, other_half, self.got))

        def fourth(self):
            line.tick()
            total = self.quadrant(column, half, self.got_b + (self.from_y,))
            height = total.shape[0] // self.lead // replicas
            self.total = total.reshape(self.lead, replicas, height, total.shape[1])
            self.halve()

        def bit(self):
            return (copy_id // self.step) % 2

        def halve(self):
            shape = self.total.shape
            pairs = self.total.reshape((self.lead, shape[1] // 2, 2) + shape[2:])
            self.own = pick(pairs, self.bit(), 2)
            self.from_z = over_z(line.mark(pick(pairs, 1 - self.bit(), 2)), self.step)

        def double(self):
            self.step //= 2
            self.from_z = over_z(self.total, self.step)

        def turn(self):
            line.tick()
            if self.halving:
                own = line.gate(self.own).astype(F32)
                self.total = line.mark((own + self.from_z.astype(F32)).astype(BF16))
                self.step *= 2
                if self.step < replicas:
                    self.halve()
                    return
                self.halving = False
                total = self.total.reshape((self.lead,) + self.total.shape[2:])
                if self.cross:
                    self.own = pick(total, core)
                    self.from_core = over_core(line.mark(pick(total, 1 - core)))
                    return
                self.total = total
                self.double()
            elif not self.crossed:
                self.crossed = True
                own, got = line.gate(self.own), self.from_core
                self.total = line.mark(self.cross(own, got))[None]
                self.double()
            elif self.step:
                self.total = line.mark(
                    jnp.where(
                        self.bit() == 0,
                        jnp.stack([line.gate(self.total), self.from_z], 1),
                        jnp.stack([self.from_z, self.total], 1),
                    ).reshape((-1,) + self.total.shape[1:])
                )
                if self.step > 1:
                    self.double()
                else:
                    self.step = 0
                    self.from_y = over_y(self.total)

        def finish(self):
            while self.step:
                self.turn()
            line.tick()
            total, got = line.gate(self.total), self.from_y
            return line.mark(
                jnp.where(half == 0, jnp.stack([total, got], 0), jnp.stack([got, total], 0)).astype(
                    F32
                )
            )

    def cross_cores(blocks):
        def exchange(own, got):
            one = own.shape[1] // blocks
            left = jnp.where(core == 0, own, got)
            right = jnp.where(core == 0, got, own)
            cols = []
            for k in range(blocks):
                cols += [left[:, k * one : (k + 1) * one], right[:, k * one : (k + 1) * one]]
            return jnp.concatenate(cols, axis=1)

        return exchange

    def by_row(left, right):
        height = owned // halves

        def quadrant(x, y, added):
            blocks = numbers(*[(x * 2 + i) * halves + y for i in range(2)])
            return line.mark(weight_grad(left, right, line.gate(blocks), height, added))

        return quadrant

    def down_quadrant(x, y, added):
        blocks = line.gate(numbers(x * halves + y))
        return line.mark(weight_grad(act_low, incoming, blocks, owned_hidden // halves, added))

    def out_quadrant(x, y, added):
        at = line.gate(numbers(x * halves + y, x, y))
        return line.mark(
            out_grad(at, mixed, branch_low, vec_grads, owned // halves, replicas, added)
        )

    pieces = halves * replicas
    total_down = Total(down_quadrant, 1, None)
    total_down.make_first()
    total_down.first()
    total_down.make_second()
    relay_down(1)
    blocks = halves * chunks
    at = [column * blocks + h for h in range(blocks)] + [place_ for _, place_ in down_others]
    hidden_low, up_sums, partial = line.mark(
        feed_back(
            line.gate(numbers(*at)),
            incoming,
            act_low,
            slope,
            down_weight,
            [value for value, _ in down_others],
        )
    )
    total_down.second()
    grad_second = line.mark(
        dot_rows(line.gate(numbers(core)), hidden_low, wup, width // 2, "grad_second")
    )
    grad_second_other = over_core(grad_second)
    total_up = Total(by_row(second_low, hidden_low), 2, cross_cores(columns))
    total_up.make_first()
    total_down.third()
    total_up.first()
    grad_middle, branch_low, sums_two = line.mark(
        norm_two_back(
            line.gate(numbers(core)), incoming, grad_second, grad_second_other, middle, gain_two
        )
    )
    grad_mixed = line.mark(
        dot_rows(line.gate(numbers(core)), branch_low, wout, width // 2, "grad_mixed")
    )
    total_up.make_second()
    grad_qkv, qv_sums = line.mark(
        attention_grad(line.gate(numbers(core)), image, qkv, grad_mixed, log_total, rows)
    )
    grad_first = line.mark(
        dot_rows(line.gate(numbers(core)), grad_qkv, wqkv, width // 2, "grad_first")
    )
    grad_first_other = over_core(grad_first)
    total_qkv = Total(by_row(first_low, grad_qkv), 2, cross_cores(3 * columns))
    total_qkv.make_first()
    total_down.fourth()
    total_up.second()
    own_grad, own_grad_low, sums_one = line.mark(
        norm_one_back(
            line.gate(numbers(core)), grad_middle, grad_first, grad_first_other, image, gain_one
        )
    )
    entries = 8 * owned + owned_hidden
    vec_grads = line.mark(
        run(
            functools.partial(pack_body, columns, owned, replicas, entries // pieces),
            "pack_vectors",
            (1,),
            line.gate(numbers(core)),
            (sums_two, sums_one, qv_sums, up_sums),
            [
                whole(8, width),
                whole(8, width),
                whole(*qv_sums.shape),
                whole(*up_sums.shape),
            ],
            [((columns, 8 * pieces, width), F32, whole(columns, 8 * pieces, width))],
        )[0]
    )
    total_out = Total(out_quadrant, 1, None)
    total_out.make_first()
    total_out.make_second()
    total_down.turn()
    total_qkv.first()
    halves_of = lambda value: value.reshape(2, padded, width)
    from_other = over_core(line.pass_on(pick(halves_of(partial), 1 - core)))
    block = pick(halves_of(middle), core) + pick(halves_of(partial), core).astype(F32)
    block = line.mark((line.gate(block) + from_other.astype(F32) + vec_down).astype(BF16))
    total_down.turn()
    total_qkv.make_second()
    total_qkv.second()
    total_qkv.third()
    total_up.third()
    total_down.turn()
    total_up.fourth()
    total_out.first()
    total_up.turn()
    total_down.turn()
    total_up.turn()
    grad_down = total_down.finish().reshape(owned_hidden, width)
    total_qkv.fourth()
    total_out.second()
    total_up.turn()
    total_up.turn()
    block_moved = swap(line.gate(block))
    total_out.third()
    total_out.fourth()
    total_qkv.turn()
    total_up.turn()
    total_qkv.turn()
    total_qkv.turn()
    total_out.turn()
    total_qkv.turn()
    moved = swap(line.gate(own_grad_low))
    total_out.turn()
    block_out = line.mark(jnp.where(half == core, line.gate(block), block_moved)[:rows][None])
    total_qkv.turn()
    total_out.turn()
    grad_up = total_up.finish().reshape(owned, up_weight.shape[1])
    token_grad = line.mark(
        jnp.where(half == core, line.gate(own_grad), moved.astype(F32))[:rows][None]
    )
    grad_qkv_w = total_qkv.finish().reshape(owned, 3 * width)
    total_out.turn()
    out_rows = total_out.finish()
    height = out_rows.shape[2] - 8
    grad_out = out_rows[:, :, :height].reshape(owned, width)

    vec_out_grads = out_rows[:, :, height, : entries // pieces].reshape(entries)
    vec_of = lambda i: vec_out_grads[i * owned : (i + 1) * owned]
    return (
        block_out,
        token_grad,
        grad_qkv_w,
        vec_of(0),
        vec_of(1),
        grad_out,
        vec_of(2),
        vec_of(3),
        vec_of(4),
        vec_of(5),
        vec_of(6),
        grad_up,
        vec_out_grads[8 * owned :],
        grad_down,
        vec_of(7),
    )


def solution(mesh):
    return jax.shard_map(
        shards,
        mesh=mesh,
        in_specs=(
            P(("shard", "rep"), "seq", None),
            P(("shard", "rep")),
            P("shard", None),
            P("shard"),
            P("shard"),
            P("shard", None),
            P("shard"),
            P("shard"),
            P("shard"),
            P("shard"),
            P("shard"),
            P("shard", None),
            P("shard"),
            P("shard", None),
            P("shard"),
            P(("shard", "rep"), "seq", None),
        ),
        out_specs=(
            P(("shard", "rep"), "seq", None),
            P(("shard", "rep"), "seq", None),
            P("shard", None),
            P("shard"),
            P("shard"),
            P("shard", None),
            P("shard"),
            P("shard"),
            P("shard"),
            P("shard"),
            P("shard"),
            P("shard", None),
            P("shard"),
            P("shard", None),
            P("shard"),
        ),
        check_vma=False,
    )
```

```python
import functools
import math

import jax
import jax.numpy as jnp
from jax import lax
from jax.experimental import pallas as pl
from jax.experimental.pallas import tpu as pltpu
from jax.sharding import PartitionSpec as P

H = 16
HD = 64
EPS = 1e-06
F32 = jnp.float32
BF16 = jnp.bfloat16
VMEM_LIMIT = 48 * 1024 * 1024
HINT = pl.CostEstimate(flops=200_000_000_000, transcendentals=0, bytes_accessed=20_000_000)


def dims(left, right, dot_left, dot_right):
    return lax.dot_general(
        left, right, (((dot_left,), (dot_right,)), ((), ())), preferred_element_type=F32
    )


def whole(*shape):
    return pl.BlockSpec(shape, lambda *index: (0,) * len(shape))


def run(body, name, grid, place, operands, in_specs, outs, scratch=()):
    return pl.pallas_call(
        body,
        grid_spec=pltpu.PrefetchScalarGridSpec(
            num_scalar_prefetch=1,
            grid=grid,
            in_specs=in_specs,
            out_specs=[out[2] for out in outs],
            scratch_shapes=list(scratch),
        ),
        out_shape=[jax.ShapeDtypeStruct(out[0], out[1]) for out in outs],
        compiler_params=pltpu.CompilerParams(vmem_limit_bytes=VMEM_LIMIT),
        cost_estimate=HINT,
        name=name,
    )(place, *operands)


def numbers(*values):
    return jnp.stack([jnp.asarray(value, jnp.int32) for value in values])


def key_visible(note_ref, padded_half, rows):
    note = note_ref[...].astype(F32)[rows % 16 : rows % 16 + 1, :]
    length = note[:, 0:1] * 16.0 + note[:, 1:2]
    row = lax.broadcasted_iota(jnp.int32, (2 * padded_half, 1), 0)
    second = row >= padded_half
    inside = jnp.where(second, row - padded_half, row)
    position = jnp.where(second, inside + rows, inside)
    return (inside < rows) & (position.astype(F32) < length)


def attend_forward(padded_half, rows, place_ref, note_ref, q_ref, k_ref, v_ref, mixed_ref, log_ref):
    visible = key_visible(note_ref, padded_half, rows)
    for head in range(2):
        lanes = slice(head * HD, (head + 1) * HD)
        scores = dims(k_ref[:, lanes], q_ref[:, lanes], 1, 1) * (HD ** -0.5)
        scores = jnp.where(visible, scores, -1000000000.0)
        top = jnp.max(scores, axis=0, keepdims=True)
        shifted = jnp.exp(scores - top)
        total = jnp.sum(shifted, axis=0, keepdims=True)
        weights = (shifted * (1.0 / total)).astype(BF16)
        log_ref[0, head : head + 1, :] = top + jnp.log(total)
        values = jnp.transpose(v_ref[:, lanes].astype(F32)).astype(BF16)
        mixed = dims(values, weights, 1, 0)
        mixed_ref[:, lanes] = jnp.transpose(mixed).astype(BF16)


def attend_backward(
    padded_half, rows, place_ref, note_ref, q_ref, k_ref, v_ref, g_ref, log_ref, out_ref, sum_ref
):
    visible = key_visible(note_ref, padded_half, rows)
    for head in range(2):
        lanes = slice(head * HD, (head + 1) * HD)
        queries, keys = q_ref[:, lanes], k_ref[:, lanes]
        values, grads = v_ref[:, lanes], g_ref[:, lanes]
        scores = dims(keys, queries, 1, 1) * (HD ** -0.5)
        weights = jnp.where(visible, jnp.exp(scores - log_ref[0, head : head + 1, :]), 0.0)
        grad_weights = dims(values, grads, 1, 1)
        inner = jnp.sum(weights * grad_weights, axis=0, keepdims=True)
        grad_scores = (weights * (grad_weights - inner)).astype(BF16)
        keys_t = jnp.transpose(keys.astype(F32)).astype(BF16)
        grad_q = (jnp.transpose(dims(keys_t, grad_scores, 1, 0)) * (HD ** -0.5)).astype(BF16)
        grad_v = dims(weights.astype(BF16), grads, 1, 0).astype(BF16)
        out_ref[0, :, lanes] = grad_q
        out_ref[1, :, lanes] = (dims(grad_scores, queries, 1, 0) * (HD ** -0.5)).astype(BF16)
        out_ref[2, :, lanes] = grad_v
        sum_ref[0, 0:1, lanes] = jnp.sum(grad_q.astype(F32), axis=0, keepdims=True)
        sum_ref[0, 1:2, lanes] = jnp.sum(grad_v.astype(F32), axis=0, keepdims=True)


def attention(place, image, qkv, rows):
    tokens, width = qkv.shape
    pairs = width // 3 // (2 * HD)
    part = lambda p: pl.BlockSpec((tokens, 2 * HD), lambda j, n, p=p: (0, p * pairs + j))
    return run(
        functools.partial(attend_forward, tokens // 2, rows),
        "attention",
        (pairs,),
        place,
        (image, qkv, qkv, qkv),
        [pl.BlockSpec((16, 128), lambda j, n: (rows // 16, 0)), part(0), part(1), part(2)],
        [
            ((tokens, width // 3), BF16, pl.BlockSpec((tokens, 2 * HD), lambda j, n: (0, j))),
            ((pairs, 2, tokens), F32, pl.BlockSpec((1, 2, tokens), lambda j, n: (j, 0, 0))),
        ],
    )


def attention_grad(place, image, qkv, grad_mixed, log_total, rows):
    tokens, width = qkv.shape
    pairs = width // 3 // (2 * HD)
    part = lambda p: pl.BlockSpec((tokens, 2 * HD), lambda j, n, p=p: (0, p * pairs + j))
    return run(
        functools.partial(attend_backward, tokens // 2, rows),
        "attention_grad",
        (pairs,),
        place,
        (image, qkv, qkv, qkv, grad_mixed, log_total),
        [
            pl.BlockSpec((16, 128), lambda j, n: (rows // 16, 0)),
            part(0),
            part(1),
            part(2),
            pl.BlockSpec((tokens, 2 * HD), lambda j, n: (0, j)),
            pl.BlockSpec((1, 2, tokens), lambda j, n: (j, 0, 0)),
        ],
        [
            (
                (3, tokens, width // 3),
                BF16,
                pl.BlockSpec((3, tokens, 2 * HD), lambda j, n: (0, 0, j)),
            ),
            ((pairs, 8, 2 * HD), F32, pl.BlockSpec((1, 8, 2 * HD), lambda j, n: (j, 0, 0))),
        ],
    )


def norm_one_body(place_ref, own_ref, other_ref, gain_ref, shift_ref, image_ref, low_ref):
    def write(values_ref):
        normal, _ = normalize(values_ref[...].astype(F32))
        image_ref[...] = values_ref[...]
        low_ref[...] = (normal * gain_ref[...] + shift_ref[...]).astype(BF16)

    mine = pl.program_id(0) == place_ref[0]
    pl.when(mine)(lambda: write(own_ref))
    pl.when(jnp.logical_not(mine))(lambda: write(other_ref))


def norm_one(place, own, other, gain, shift):
    padded, width = own.shape
    rows = pl.BlockSpec((padded, width), lambda i, n: (i, 0))
    shape = (2 * padded, width)
    return run(
        norm_one_body,
        "norm_one",
        (2,),
        place,
        (own, other, gain, shift),
        [whole(padded, width)] * 2 + [whole(1, width)] * 2,
        [(shape, BF16, rows)] * 2,
    )


def norm_two_body(
    place_ref, image_ref, own_ref, other_ref, bias_ref, gain_ref, shift_ref, middle_ref, low_ref
):
    branch = own_ref[...].astype(F32) + other_ref[...].astype(F32)
    middle = image_ref[...].astype(F32) + branch + bias_ref[...]
    normal, _ = normalize(middle)
    middle_ref[...] = middle
    low_ref[...] = (normal * gain_ref[...] + shift_ref[...]).astype(BF16)


def norm_two(place, image, own, other, bias, gain, shift):
    tokens, width = image.shape
    rows = pl.BlockSpec((tokens // 2, width), lambda i, n: (i, 0))
    return run(
        norm_two_body,
        "norm_two",
        (2,),
        place,
        (image, own, other, bias, gain, shift),
        [rows] * 3 + [whole(1, width)] * 3,
        [((tokens, width), F32, rows), ((tokens, width), BF16, rows)],
    )


def add_sums(sum_ref, values):
    @pl.when(pl.program_id(0) == 0)
    def _():
        sum_ref[...] = jnp.zeros_like(sum_ref)

    for k, value in enumerate(values):
        sum_ref[k : k + 1, :] += jnp.sum(value, axis=0, keepdims=True)


def norm_two_back_body(
    place_ref, incoming_ref, own_ref, other_ref, middle_ref, gain_ref, grad_ref, low_ref, sum_ref
):
    incoming = incoming_ref[...].astype(F32)
    grad = own_ref[...].astype(F32) + other_ref[...].astype(F32)
    normal, scale = normalize(middle_ref[...])
    grad_middle = incoming + normalize_grad(grad, gain_ref[...], normal, scale)
    low = grad_middle.astype(BF16)
    grad_ref[...] = grad_middle
    low_ref[...] = low
    add_sums(sum_ref, (grad * normal, grad, low.astype(F32), incoming))


def norm_two_back(place, incoming, own, other, middle, gain):
    tokens, width = incoming.shape
    rows = pl.BlockSpec((tokens // 2, width), lambda i, n: (i, 0))
    return run(
        norm_two_back_body,
        "norm_two_back",
        (2,),
        place,
        (incoming, own, other, middle, gain),
        [rows] * 4 + [whole(1, width)],
        [((tokens, width), F32, rows), ((tokens, width), BF16, rows), ((8, width), F32, whole(8, width))],
    )


def norm_one_back_body(
    place_ref, grad_ref, own_ref, other_ref, image_ref, gain_ref, kept_ref, low_ref, sum_ref
):
    grad = own_ref[...].astype(F32) + other_ref[...].astype(F32)
    normal, scale = normalize(image_ref[...].astype(F32))
    total = grad_ref[...] + normalize_grad(grad, gain_ref[...], normal, scale)
    add_sums(sum_ref, (grad * normal, grad))

    @pl.when(pl.program_id(0) == place_ref[0])
    def _():
        kept_ref[...] = total
        low_ref[...] = total.astype(BF16)


def norm_one_back(place, grad_middle, own, other, image, gain):
    tokens, width = image.shape
    padded = tokens // 2
    rows = pl.BlockSpec((padded, width), lambda i, n: (i, 0))
    return run(
        norm_one_back_body,
        "norm_one_back",
        (2,),
        place,
        (grad_middle, own, other, image, gain),
        [rows] * 4 + [whole(1, width)],
        [
            ((padded, width), F32, whole(padded, width)),
            ((padded, width), BF16, whole(padded, width)),
            ((8, width), F32, whole(8, width)),
        ],
    )


def split_body(part_rows, place_ref, keep_in, send_in, keep, send, *parts):
    keep[...] = keep_in[...]
    send[...] = send_in[...]
    if parts:
        first = pl.multiple_of(place_ref[1] * part_rows, part_rows)
        parts[0][...] = keep_in[pl.ds(first, part_rows), :]
        parts[1][...] = send_in[pl.ds(first, part_rows), :]


def split_columns(place, shard, number, part_rows, name):
    depth, wide = shard.shape
    one = wide // number // 2
    out = lambda rows: ((rows, wide // 2), BF16, pl.BlockSpec((rows, one), lambda j, n: (0, j)))
    return run(
        functools.partial(split_body, part_rows),
        name,
        (number,),
        place,
        (shard, shard),
        [
            pl.BlockSpec((depth, one), lambda j, n: (0, 2 * j + n[0])),
            pl.BlockSpec((depth, one), lambda j, n: (0, 2 * j + 1 - n[0])),
        ],
        [out(depth)] * 2 + ([out(part_rows)] * 2 if part_rows else []),
    )


def pair_body(rows, place_ref, own_ref, other_ref, out_ref):
    first = pl.multiple_of(place_ref[1] * rows, rows)
    zero = place_ref[0] == 0
    own, other = own_ref[pl.ds(first, rows), :], other_ref[pl.ds(first, rows), :]
    out_ref[:rows, :] = jnp.where(zero, own, other)
    out_ref[rows:, :] = jnp.where(zero, other, own)


def pair_part(place, own, other, rows):
    depth, wide = own.shape
    tile = wide // 2
    return run(
        functools.partial(pair_body, rows),
        "pair_part",
        (2,),
        place,
        (own, other),
        [pl.BlockSpec((depth, tile), lambda j, n: (0, j))] * 2,
        [((2 * rows, wide), BF16, pl.BlockSpec((2 * rows, tile), lambda j, n: (0, j)))],
    )[0]


def join_body(blocks, count, finish, place_ref, left_ref, bias_ref, *refs):
    pieces, joined_ref, outs = refs[:count], refs[count], refs[count + 1 :]
    for k, (number, source, rows) in enumerate(blocks):
        first = pl.multiple_of(place_ref[k] * rows, rows)
        joined_ref[pl.ds(first, rows), :] = pieces[number][source : source + rows, :]
    total = dims(left_ref[...], joined_ref[...], 1, 0) + bias_ref[...]
    for out, value in zip(outs, finish(total)):
        out[...] = value.astype(out.dtype)


def join_dot(line, left, pieces, bias, finish, results, tile, name):
    arrays = []
    for piece in pieces:
        if not any(piece[0] is array for array in arrays):
            arrays.append(piece[0])
    number = lambda array: [array is other for other in arrays].index(True)
    blocks = [(number(array), source, rows) for array, source, rows, _ in pieces]
    place = line.gate(numbers(*[piece[3] for piece in pieces]))
    tokens, depth = left.shape
    wide = arrays[0].shape[1]
    spec = lambda rows: pl.BlockSpec((rows, tile), lambda j, n: (0, j))
    return line.mark(
        run(
            functools.partial(join_body, blocks, len(arrays), finish),
            name,
            (wide // tile,),
            place,
            (left, bias) + tuple(arrays),
            [whole(tokens, depth), spec(1)] + [spec(array.shape[0]) for array in arrays],
            [((depth, wide), BF16, spec(depth))] + [((tokens, wide), BF16, spec(tokens))] * results,
        )
    )


def activate(hidden):
    normal = 0.5 * (1.0 + lax.erf(hidden * math.sqrt(0.5)))
    density = jnp.exp(-0.5 * hidden * hidden) * (1.0 / math.sqrt(2.0 * math.pi))
    return hidden * normal, normal + hidden * density


def feed_back_body(
    own_blocks, count, place_ref, incoming_ref, act_ref, slope_ref, own_ref, *refs
):
    others, (low_ref, sum_ref, part_ref), (weight_ref, total_ref) = (
        refs[:count],
        refs[count : count + 3],
        refs[count + 3 :],
    )
    step = pl.program_id(0)

    @pl.when(step < own_blocks)
    def _():
        weight_ref[...] = own_ref[...]

    for k in range(count):

        @pl.when(step == own_blocks + k)
        def _(k=k):
            weight_ref[...] = others[k][...]

    grad = dims(incoming_ref[...], weight_ref[...], 1, 1) * slope_ref[...].astype(F32)
    low = grad.astype(BF16)
    low_ref[...] = low
    sum_ref[...] = jnp.sum(low.astype(F32), axis=0, keepdims=True)
    part = dims(act_ref[...], weight_ref[...], 1, 0)
    total = jnp.where(step == 0, part, total_ref[...] + part)
    total_ref[...] = total

    @pl.when(step == own_blocks + count - 1)
    def _():
        part_ref[...] = total.astype(BF16)


def feed_back(place, incoming, act, slope, own, others):
    tokens, width = incoming.shape
    hidden = act.shape[1]
    tile = others[0].shape[0]
    own_blocks = own.shape[0] // tile
    steps = own_blocks + len(others)
    block = pl.BlockSpec((tokens, tile), lambda s, n: (0, n[s]))
    return run(
        functools.partial(feed_back_body, own_blocks, len(others)),
        "feed_back",
        (steps,),
        place,
        (incoming, act, slope, own) + tuple(others),
        [
            whole(tokens, width),
            block,
            block,
            pl.BlockSpec((tile, width), lambda s, n: (jnp.minimum(s, own_blocks - 1), 0)),
        ]
        + [whole(tile, width)] * len(others),
        [
            ((tokens, hidden), BF16, block),
            ((1, hidden), F32, pl.BlockSpec((1, tile), lambda s, n: (0, n[s]))),
            ((tokens, width), BF16, whole(tokens, width)),
        ],
        [pltpu.VMEM((tile, width), BF16), pltpu.VMEM((tokens, width), F32)],
    )


def dot_rows_body(place_ref, left_ref, weight_ref, out_ref):
    parts = left_ref.shape[0] if len(left_ref.shape) == 3 else 1
    if parts == 1:
        total = dims(left_ref[...], weight_ref[...], 1, 1)
    else:
        one = left_ref.shape[2]
        total = dims(left_ref[0], weight_ref[:, :one], 1, 1)
        for p in range(1, parts):
            total = total + dims(left_ref[p], weight_ref[:, p * one : (p + 1) * one], 1, 1)
    out_ref[...] = total.astype(BF16)


def dot_rows(place, left, weight, tile, name):
    tokens = left.shape[-2]
    rows, depth = weight.shape
    return run(
        dot_rows_body,
        name,
        (rows // tile,),
        place,
        (left, weight),
        [whole(*left.shape), pl.BlockSpec((tile, depth), lambda j, n: (j, 0))],
        [((tokens, rows), BF16, pl.BlockSpec((tokens, tile), lambda j, n: (0, j)))],
    )[0]


def pack_body(columns, owned, replicas, share, place_ref, two_ref, one_ref, qv_ref, up_ref, out_ref):
    zero = place_ref[0] == 0
    pairs = qv_ref.shape[0] // columns
    hidden = up_ref.shape[1] // columns
    out_ref[...] = jnp.zeros_like(out_ref)
    for x in range(columns):
        parts = [qv_ref[x * pairs + p, row : row + 1, :] for row in range(2) for p in range(pairs)]
        for ref, row in ((two_ref, 2), (one_ref, 0), (one_ref, 1), (two_ref, 0), (two_ref, 1), (two_ref, 3)):
            first, second = (
                ref[row : row + 1, (2 * x + c) * owned : (2 * x + c + 1) * owned] for c in range(2)
            )
            parts.append(jnp.where(zero, first, second))
        parts.append(up_ref[:, x * hidden : (x + 1) * hidden])
        row = jnp.concatenate(parts, axis=1)
        for p in range(out_ref.shape[1] // 8):
            out_ref[x, 8 * p : 8 * p + 1, :share] = row[:, p * share : (p + 1) * share]


def out_grad_body(count, replicas, place_ref, left_ref, right_ref, vec_ref, *rest):
    total = dims(left_ref[...], right_ref[...], 0, 0)
    height = total.shape[0] // replicas
    every = height + 8
    for z in range(replicas):
        for first, value in (
            (z * every, total[z * height : (z + 1) * height]),
            (z * every + height, vec_ref[0, 8 * z : 8 * z + 8, :]),
        ):
            rows = slice(first, first + value.shape[0])
            for added in rest[:count]:
                value = value + added[rows, :].astype(F32)
            rest[count][rows, :] = value.astype(BF16)


def out_grad(place, left, right, vectors, height, replicas, added=()):
    tokens, width = right.shape
    every = height + 8 * replicas
    if height % 128:
        left = lax.dynamic_slice_in_dim(left, place[0] * height, height, 1)
        place = place * numbers(0, 1, 1)
    return run(
        functools.partial(out_grad_body, len(added), replicas),
        "out_grad",
        (1,),
        place,
        (left, right, vectors) + tuple(added),
        [
            pl.BlockSpec((tokens, height), lambda i, n: (0, n[0])),
            whole(tokens, width),
            pl.BlockSpec((1, 8 * replicas, width), lambda i, n: (n[1], n[2], 0)),
        ]
        + [whole(every, width)] * len(added),
        [((every, width), BF16, whole(every, width))],
    )[0]


def weight_grad_body(count, index_ref, left_ref, right_ref, *rest):
    total = dims(left_ref[...], right_ref[...], 0, 0)
    for added in rest[:count]:
        total = total + added[...].astype(F32)
    rest[count][...] = total.astype(BF16)


def weight_grad(left, right, blocks, height, added=()):
    tokens = left.shape[0]
    number = blocks.shape[0]
    if height % 128:
        narrow = [
            lax.dynamic_slice_in_dim(left, blocks[i] * height, height, 1) for i in range(number)
        ]
        left = jnp.concatenate(narrow, axis=1)
        blocks = jnp.zeros((1,), jnp.int32)
        number, height = 1, number * height
    parts = right.shape[0] if right.ndim == 3 else 1
    width = right.shape[-1]
    if right.ndim == 3:
        right_spec = pl.BlockSpec((pl.Squeezed(), tokens, width), lambda i, j, n: (j, 0, 0))
    else:
        parts = 2
        width = width // parts
        right_spec = pl.BlockSpec((tokens, width), lambda i, j, n: (0, j))
    tile = pl.BlockSpec((height, width), lambda i, j, n: (i, j))
    return pl.pallas_call(
        functools.partial(weight_grad_body, len(added)),
        grid_spec=pltpu.PrefetchScalarGridSpec(
            num_scalar_prefetch=1,
            grid=(number, parts),
            in_specs=[pl.BlockSpec((tokens, height), lambda i, j, n: (0, n[i])), right_spec]
            + [tile] * len(added),
            out_specs=tile,
        ),
        out_shape=jax.ShapeDtypeStruct((number * height, parts * width), BF16),
        compiler_params=pltpu.CompilerParams(vmem_limit_bytes=VMEM_LIMIT),
        cost_estimate=HINT,
        name="weight_grad",
    )(blocks, left, right, *added)


def tick_body(place_ref, out_ref):
    out_ref[...] = jnp.full(out_ref.shape, place_ref[0], jnp.int32)


class Line:
    def __init__(self):
        self.last = None

    def gate(self, value):
        if self.last is None:
            return value
        return lax.optimization_barrier((value, self.last))[0]

    def mark(self, value):
        self.last = value
        return value

    def tick(self):
        place = self.gate(jnp.zeros((1,), jnp.int32))
        self.last = run(
            tick_body, "tick", (1,), place, (), [], [((8, 128), jnp.int32, whole(8, 128))]
        )[0]

    def pass_on(self, value):
        self.tick()
        return self.mark(self.gate(value))


def normalize(values):
    centered = values - jnp.mean(values, -1, keepdims=True)
    scale = lax.rsqrt(jnp.mean(centered * centered, -1, keepdims=True) + EPS)
    return centered * scale, scale


def normalize_grad(grad, gain, normal, scale):
    scaled = grad * gain
    return scale * (
        scaled
        - jnp.mean(scaled, -1, keepdims=True)
        - normal * jnp.mean(scaled * normal, -1, keepdims=True)
    )


def place(buffer, piece, position):
    start = (position,) + (0,) * (buffer.ndim - 1)
    return lax.dynamic_update_slice(buffer, piece[None], start)


def pick(array, index, axis=0):
    return lax.dynamic_index_in_dim(array, index, axis, keepdims=False)


def shards(
    tokens,
    lengths,
    qkv_weight,
    query_bias,
    value_bias,
    out_weight,
    out_bias,
    first_gain,
    first_shift,
    second_gain,
    second_shift,
    up_weight,
    up_bias,
    down_weight,
    down_bias,
    cotangent,
):
    _, rows, width = tokens.shape
    halves = lax.axis_size("seq")
    group = lax.axis_size("shard")
    replicas = lax.axis_size("rep")
    columns = group // 2
    half, member, copy_id = (lax.axis_index(name) for name in ("seq", "shard", "rep"))
    core, column = member % 2, member // 2
    owned = width // group
    owned_hidden = up_bias.shape[0]
    padded = -(-(rows + 1) // 16) * 16

    def over_core(value):
        return lax.ppermute(value, "shard", [(i, i ^ 1) for i in range(group)])

    def over_x(value, step):
        return lax.ppermute(value, "shard", [(i, (i + 2 * step) % group) for i in range(group)])

    def over_x_core(value, step):
        pairs = [(i, ((i + 2 * step) % group) ^ 1) for i in range(group)]
        return lax.ppermute(value, "shard", pairs)

    def over_y(value):
        return lax.ppermute(value, "seq", [(i, halves - 1 - i) for i in range(halves)])

    def over_z(value, step):
        return lax.ppermute(value, "rep", [(i, i ^ step) for i in range(replicas)])

    swaps = []
    for s in range(halves):
        for h in range(group):
            if s != h % 2:
                swaps.append((s * group + h, (h % 2) * group + (h // 2) * 2 + s))

    def swap(value):
        return lax.ppermute(value, ("seq", "shard"), swaps)

    def by_core(mine, other, axis=0):
        return jnp.where(
            core == 0, jnp.stack([mine, other], axis), jnp.stack([other, mine], axis)
        )

    line = Line()
    steps = range(1, columns)
    other_half = halves - 1 - half
    side = copy_id % 2
    quarter = half * 2 + side

    length = lengths[0]
    lane = lax.broadcasted_iota(jnp.int32, (padded - rows, width), 1)
    note = jnp.where(lane == 0, length // 16, jnp.where(lane == 1, length % 16, 0)).astype(BF16)
    own_half = lambda shard: pick(
        shard.reshape(halves, shard.shape[0] // halves, shard.shape[1]), half
    )
    source = lambda k: (column - k) % columns
    part = owned // halves
    eighth = owned // halves // 2
    chunks = 2

    def relay_qkv(index, c):
        for k in steps:
            value = line.pass_on(qkv_x[index][k - 1])
            at = (2 * source(k) + c) * halves
            qkv_pieces.append((value, 0, part, at + half))
            qkv_pieces.append((over_y(value), 0, part, at + other_half))

    qkv_x = {}

    own_tokens = line.mark(jnp.concatenate([line.gate(tokens[0]), note], axis=0))
    other_tokens = swap(own_tokens)
    singles = [
        query_bias,
        value_bias,
        out_bias,
        first_gain,
        first_shift,
        second_gain,
        second_shift,
        down_bias,
    ]
    singles += [up_bias[i * owned : (i + 1) * owned] for i in range(owned_hidden // owned)]
    row_of = lax.broadcasted_iota(jnp.int32, (16, owned), 0)
    vectors = jnp.zeros((16, owned), BF16)
    for i, single in enumerate(singles):
        vectors = jnp.where(row_of == i, jnp.broadcast_to(single[None], (16, owned)), vectors)
    vectors = line.mark(line.gate(vectors))
    vec_x = [over_x(vectors, k) for k in steps]
    qkv_keep, qkv_send, qkv_part, qkv_cross = line.mark(
        split_columns(
            line.gate(numbers(core, half)), qkv_weight, 3 * columns, owned // halves, "split_qkv"
        )
    )
    qkv_x[0] = [over_x(qkv_part, k) for k in steps]
    qkv_x[1] = [over_x_core(line.gate(qkv_cross), k) for k in steps]
    qkv_core = over_core(line.gate(qkv_send))
    qkv_core = line.pass_on(qkv_core)
    qkv_pieces = [
        (qkv_keep, 0, owned, member),
        (qkv_core, 0, owned, member + 1 - 2 * core),
    ]
    relay_qkv(0, core)
    own_image = line.mark(jnp.where(half == core, own_tokens, line.pass_on(other_tokens)))
    other_image = over_core(own_image)
    other_image = line.pass_on(other_image)
    up_keep, up_send = line.mark(
        split_columns(line.gate(numbers(core, half)), up_weight, columns, 0, "split_up")
    )
    gathered_vec = jnp.zeros((columns,) + vectors.shape, BF16)
    gathered_vec = place(gathered_vec, vectors, column)
    for k in steps:
        gathered_vec = place(gathered_vec, line.pass_on(vec_x[k - 1]), (column - k) % columns)
    line.mark(gathered_vec)
    vec_core = over_core(gathered_vec)
    up_core = over_core(line.gate(up_send))
    up_core = line.pass_on(up_core)
    up_part = line.mark(pair_part(line.gate(numbers(core, quarter)), up_keep, up_core, eighth))
    out_part = line.mark(own_half(line.gate(out_weight)))
    out_x = [over_x(line.gate(out_part), k) for k in steps]
    vec_core = line.pass_on(vec_core)
    mine_vec = gathered_vec.astype(F32)
    all_vec = by_core(gathered_vec, vec_core, 1).reshape(columns * 2, 16, owned)
    all_vec = all_vec.astype(F32)
    vec = lambda i: all_vec[:, i].reshape(1, width)
    own_vec = lambda i: mine_vec[:, i].reshape(1, width // 2)
    gain_one, shift_one, gain_two, shift_two = vec(3), vec(4), vec(5), vec(6)
    vec_out, vec_down = vec(2), vec(7)
    vec_up = mine_vec[:, 8 : 8 + owned_hidden // owned].reshape(1, columns * owned_hidden)
    vec_qkv = jnp.concatenate(
        [own_vec(0), jnp.zeros((1, width // 2), F32), own_vec(1)], axis=1
    )
    up_x = [over_x(line.gate(up_part), k) for k in steps]
    image, first_low = line.mark(
        norm_one(line.gate(numbers(core)), own_image, other_image, gain_one, shift_one)
    )
    own_cotangent = line.mark(
        jnp.concatenate([line.gate(cotangent[0]), jnp.zeros((padded - rows, width), BF16)], axis=0)
    )
    down_part = line.mark(own_half(line.gate(down_weight)).reshape(chunks, -1, width))
    relay_qkv(1, 1 - core)
    out_pieces = [(out_weight, 0, owned, column)]
    for k in steps:
        value = line.pass_on(out_x[k - 1])
        at = source(k) * halves
        out_pieces += [(value, 0, part, at + half), (over_y(value), 0, part, at + other_half)]
    down_x = [[over_x(line.gate(down_part[0]), k) for k in steps]]
    wqkv, qkv = join_dot(
        line, first_low, qkv_pieces, vec_qkv, lambda total: (total,), 1, width // 2, "project"
    )

    up_pieces = [(up_keep, 0, owned, member), (up_core, 0, owned, member + 1 - 2 * core)]

    def up_rows(value, k, h, s):
        for c in range(2):
            at = (2 * source(k) + c) * halves * 2 + h * 2 + s
            up_pieces.append((value, c * eighth, eighth, at))

    up_y, up_z, down_others = [], [], []
    no_bias = jnp.zeros((1, width), F32)

    def relay_down(c):
        for k in steps:
            value = line.pass_on(down_x[c][k - 1])
            at = source(k) * halves * chunks + c
            down_others.append((value, at + half * chunks))
            down_others.append((over_y(value), at + other_half * chunks))

    for k in steps:
        value = line.pass_on(up_x[k - 1])
        up_rows(value, k, half, side)
        up_z.append(over_z(value, 1))
        up_y.append(over_y(value))
    mixed, log_total = line.mark(attention(line.gate(numbers(core)), image, qkv, rows))
    wout, branch = join_dot(
        line, mixed, out_pieces, no_bias, lambda total: (total,), 1, width // 2, "project_out"
    )
    branch_other = over_core(branch)
    other_cotangent = swap(line.gate(own_cotangent))
    for k in steps:
        value = line.pass_on(up_y[k - 1])
        up_rows(value, k, other_half, side)
        up_y[k - 1] = over_z(value, 1)
    relay_down(0)
    for k in steps:
        up_rows(line.pass_on(up_z[k - 1]), k, half, 1 - side)
    line.tick()
    down_x.append([over_x(line.gate(down_part[1]), k) for k in steps])
    middle, second_low = line.mark(
        norm_two(
            line.gate(numbers(core)), image, branch, branch_other, vec_out, gain_two, shift_two
        )
    )
    other_cotangent = line.pass_on(other_cotangent)
    own_incoming = line.mark(jnp.where(half == core, own_cotangent, other_cotangent))
    incoming_other = over_core(own_incoming)
    incoming_other = line.pass_on(incoming_other)
    incoming = line.mark(by_core(own_incoming, incoming_other).reshape(2 * padded, width))
    for k in steps:
        up_rows(line.pass_on(up_y[k - 1]), k, other_half, 1 - side)
    wup, act_low, slope = join_dot(line, second_low, up_pieces, vec_up, activate, 2, 512, "hidden")

    class Total:
        def __init__(self, quadrant, lead, cross, split=False):
            self.quadrant, self.lead, self.cross, self.split = quadrant, lead, cross, split
            self.crossed = not cross
            self.halving, self.done, self.step = True, False, 1

        def along_x(self, y):
            return [self.quadrant((column + k) % columns, y, ()) for k in steps]

        def make_first(self):
            self.sent = self.along_x(other_half)

        def make_second(self):
            self.sent_b = self.along_x(half)

        def first(self):
            self.got = tuple(over_x(line.gate(v), k) for k, v in zip(steps, self.sent))

        def second(self):
            self.got_b = tuple(over_x(line.gate(v), k) for k, v in zip(steps, self.sent_b))

        def third(self):
            line.tick()
            self.from_y = over_y(self.quadrant(column, other_half, self.got))

        def fourth(self):
            line.tick()
            total = self.quadrant(column, half, self.got_b + (self.from_y,))
            height = total.shape[0] // self.lead // replicas
            self.total = total.reshape(self.lead, replicas, height, total.shape[1])
            self.halve()

        def bit(self):
            return (copy_id // self.step) % 2

        def halve(self):
            shape = self.total.shape
            pairs = self.total.reshape((self.lead, shape[1] // 2, 2) + shape[2:])
            self.own = pick(pairs, self.bit(), 2)
            self.from_z = over_z(line.mark(pick(pairs, 1 - self.bit(), 2)), self.step)

        def double(self):
            self.step //= 2
            self.from_z = over_z(self.total, self.step)
            if self.split and self.step == 1:
                self.early = over_y(self.total)

        def joined(self, own, got):
            return jnp.where(
                self.bit() == 0, jnp.stack([own, got], 1), jnp.stack([got, own], 1)
            ).reshape((-1,) + own.shape[1:])

        def turn(self):
            line.tick()
            if self.halving:
                own = line.gate(self.own).astype(F32)
                self.total = line.mark((own + self.from_z.astype(F32)).astype(BF16))
                self.step *= 2
                if self.step < replicas:
                    self.halve()
                    return
                self.halving = False
                total = self.total.reshape((self.lead,) + self.total.shape[2:])
                if self.cross:
                    self.own = pick(total, core)
                    self.from_core = over_core(line.mark(pick(total, 1 - core)))
                    return
                self.total = total
                self.double()
            elif not self.crossed:
                self.crossed = True
                own, got = line.gate(self.own), self.from_core
                self.total = line.mark(self.cross(own, got))[None]
                self.double()
            elif self.step:
                if self.split and self.step == 1:
                    self.from_z = line.mark(line.gate(self.from_z))
                    late = over_y(self.from_z)
                    self.total = self.joined(self.total, self.from_z)
                    self.from_y = self.joined(self.early, late)
                    self.step = 0
                    return
                self.total = line.mark(self.joined(line.gate(self.total), self.from_z))
                if self.step > 1:
                    self.double()
                else:
                    self.step = 0
                    self.from_y = over_y(self.total)

        def finish(self):
            while self.step:
                self.turn()
            line.tick()
            total, got = line.gate(self.total), self.from_y
            return line.mark(
                jnp.where(half == 0, jnp.stack([total, got], 0), jnp.stack([got, total], 0)).astype(
                    F32
                )
            )

    def cross_cores(blocks):
        def exchange(own, got):
            one = own.shape[1] // blocks
            left = jnp.where(core == 0, own, got)
            right = jnp.where(core == 0, got, own)
            cols = []
            for k in range(blocks):
                cols += [left[:, k * one : (k + 1) * one], right[:, k * one : (k + 1) * one]]
            return jnp.concatenate(cols, axis=1)

        return exchange

    def by_row(left, right):
        height = owned // halves

        def quadrant(x, y, added):
            blocks = numbers(*[(x * 2 + i) * halves + y for i in range(2)])
            return line.mark(weight_grad(left, right, line.gate(blocks), height, added))

        return quadrant

    def down_quadrant(x, y, added):
        blocks = line.gate(numbers(x * halves + y))
        return line.mark(weight_grad(act_low, incoming, blocks, owned_hidden // halves, added))

    def out_quadrant(x, y, added):
        at = line.gate(numbers(x * halves + y, x, y))
        return line.mark(
            out_grad(at, mixed, branch_low, vec_grads, owned // halves, replicas, added)
        )

    pieces = halves * replicas
    total_down = Total(down_quadrant, 1, None)
    total_down.make_first()
    total_down.first()
    total_down.make_second()
    relay_down(1)
    blocks = halves * chunks
    at = [column * blocks + h for h in range(blocks)] + [place_ for _, place_ in down_others]
    hidden_low, up_sums, partial = line.mark(
        feed_back(
            line.gate(numbers(*at)),
            incoming,
            act_low,
            slope,
            down_weight,
            [value for value, _ in down_others],
        )
    )
    total_down.second()
    grad_second = line.mark(
        dot_rows(line.gate(numbers(core)), hidden_low, wup, width // 2, "grad_second")
    )
    grad_second_other = over_core(grad_second)
    total_up = Total(by_row(second_low, hidden_low), 2, cross_cores(columns), True)
    total_up.make_first()
    total_down.third()
    total_up.first()
    grad_middle, branch_low, sums_two = line.mark(
        norm_two_back(
            line.gate(numbers(core)), incoming, grad_second, grad_second_other, middle, gain_two
        )
    )
    grad_mixed = line.mark(
        dot_rows(line.gate(numbers(core)), branch_low, wout, width // 2, "grad_mixed")
    )
    grad_qkv, qv_sums = line.mark(
        attention_grad(line.gate(numbers(core)), image, qkv, grad_mixed, log_total, rows)
    )
    grad_first = line.mark(
        dot_rows(line.gate(numbers(core)), grad_qkv, wqkv, width // 2, "grad_first")
    )
    grad_first_other = over_core(grad_first)
    total_qkv = Total(by_row(first_low, grad_qkv), 2, cross_cores(3 * columns), True)
    total_qkv.make_first()
    total_down.fourth()
    total_up.make_second()
    total_up.second()
    own_grad, own_grad_low, sums_one = line.mark(
        norm_one_back(
            line.gate(numbers(core)), grad_middle, grad_first, grad_first_other, image, gain_one
        )
    )
    entries = 8 * owned + owned_hidden
    vec_grads = line.mark(
        run(
            functools.partial(pack_body, columns, owned, replicas, entries // pieces),
            "pack_vectors",
            (1,),
            line.gate(numbers(core)),
            (sums_two, sums_one, qv_sums, up_sums),
            [
                whole(8, width),
                whole(8, width),
                whole(*qv_sums.shape),
                whole(*up_sums.shape),
            ],
            [((columns, 8 * pieces, width), F32, whole(columns, 8 * pieces, width))],
        )[0]
    )
    total_out = Total(out_quadrant, 1, None)
    total_out.make_first()
    total_qkv.make_second()
    total_out.make_second()
    total_down.turn()
    total_qkv.first()
    halves_of = lambda value: value.reshape(2, padded, width)
    from_other = over_core(line.pass_on(pick(halves_of(partial), 1 - core)))
    block = pick(halves_of(middle), core) + pick(halves_of(partial), core).astype(F32)
    block = line.mark((line.gate(block) + from_other.astype(F32) + vec_down).astype(BF16))
    total_down.turn()
    total_qkv.second()
    total_qkv.third()
    total_up.third()
    total_down.turn()
    total_up.fourth()
    total_out.first()
    total_up.turn()
    total_down.turn()
    total_up.turn()
    grad_down = total_down.finish().reshape(owned_hidden, width)
    total_qkv.fourth()
    total_up.turn()
    total_up.turn()
    block_moved = swap(line.gate(block))
    total_out.second()
    total_out.third()
    total_out.fourth()
    total_qkv.turn()
    total_up.turn()
    total_qkv.turn()
    total_qkv.turn()
    total_out.turn()
    total_qkv.turn()
    moved = swap(line.gate(own_grad_low))
    total_out.turn()
    total_qkv.turn()
    total_out.turn()
    block_out = line.mark(jnp.where(half == core, line.gate(block), block_moved)[:rows][None])
    grad_qkv_w = total_qkv.finish().reshape(owned, 3 * width)
    total_out.turn()
    out_rows = total_out.finish()
    height = out_rows.shape[2] - 8
    grad_out = out_rows[:, :, :height].reshape(owned, width)
    token_grad = line.mark(
        jnp.where(half == core, line.gate(own_grad), moved.astype(F32))[:rows][None]
    )
    grad_up = total_up.finish().reshape(owned, up_weight.shape[1])

    vec_out_grads = out_rows[:, :, height, : entries // pieces].reshape(entries)
    vec_of = lambda i: vec_out_grads[i * owned : (i + 1) * owned]
    return (
        block_out,
        token_grad,
        grad_qkv_w,
        vec_of(0),
        vec_of(1),
        grad_out,
        vec_of(2),
        vec_of(3),
        vec_of(4),
        vec_of(5),
        vec_of(6),
        grad_up,
        vec_out_grads[8 * owned :],
        grad_down,
        vec_of(7),
    )


def solution(mesh):
    return jax.shard_map(
        shards,
        mesh=mesh,
        in_specs=(
            P(("shard", "rep"), "seq", None),
            P(("shard", "rep")),
            P("shard", None),
            P("shard"),
            P("shard"),
            P("shard", None),
            P("shard"),
            P("shard"),
            P("shard"),
            P("shard"),
            P("shard"),
            P("shard", None),
            P("shard"),
            P("shard", None),
            P("shard"),
            P(("shard", "rep"), "seq", None),
        ),
        out_specs=(
            P(("shard", "rep"), "seq", None),
            P(("shard", "rep"), "seq", None),
            P("shard", None),
            P("shard"),
            P("shard"),
            P("shard", None),
            P("shard"),
            P("shard"),
            P("shard"),
            P("shard"),
            P("shard"),
            P("shard", None),
            P("shard"),
            P("shard", None),
            P("shard"),
        ),
        check_vma=False,
    )
```

```python
import functools
import math

import jax
import jax.numpy as jnp
from jax import lax
from jax.experimental import pallas as pl
from jax.experimental.pallas import tpu as pltpu
from jax.sharding import PartitionSpec as P

H = 16
HD = 64
EPS = 1e-06
F32 = jnp.float32
BF16 = jnp.bfloat16
VMEM_LIMIT = 48 * 1024 * 1024
HINT = pl.CostEstimate(flops=200_000_000_000, transcendentals=0, bytes_accessed=20_000_000)


def dims(left, right, dot_left, dot_right):
    return lax.dot_general(
        left, right, (((dot_left,), (dot_right,)), ((), ())), preferred_element_type=F32
    )


def whole(*shape):
    return pl.BlockSpec(shape, lambda *index: (0,) * len(shape))


def run(body, name, grid, place, operands, in_specs, outs, scratch=()):
    return pl.pallas_call(
        body,
        grid_spec=pltpu.PrefetchScalarGridSpec(
            num_scalar_prefetch=1,
            grid=grid,
            in_specs=in_specs,
            out_specs=[out[2] for out in outs],
            scratch_shapes=list(scratch),
        ),
        out_shape=[jax.ShapeDtypeStruct(out[0], out[1]) for out in outs],
        compiler_params=pltpu.CompilerParams(vmem_limit_bytes=VMEM_LIMIT),
        cost_estimate=HINT,
        name=name,
    )(place, *operands)


def numbers(*values):
    return jnp.stack([jnp.asarray(value, jnp.int32) for value in values])


def key_visible(note_ref, padded_half, rows):
    note = note_ref[...].astype(F32)[rows % 16 : rows % 16 + 1, :]
    length = note[:, 0:1] * 16.0 + note[:, 1:2]
    row = lax.broadcasted_iota(jnp.int32, (2 * padded_half, 1), 0)
    second = row >= padded_half
    inside = jnp.where(second, row - padded_half, row)
    position = jnp.where(second, inside + rows, inside)
    return (inside < rows) & (position.astype(F32) < length)


def attend_forward(padded_half, rows, place_ref, note_ref, q_ref, k_ref, v_ref, mixed_ref, log_ref):
    visible = key_visible(note_ref, padded_half, rows)
    for head in range(2):
        lanes = slice(head * HD, (head + 1) * HD)
        scores = dims(k_ref[:, lanes], q_ref[:, lanes] * (HD ** -0.5), 1, 1)
        scores = jnp.where(visible, scores, -1000000000.0)
        top = jnp.max(scores, axis=0, keepdims=True)
        shifted = jnp.exp(scores - top)
        total = jnp.sum(shifted, axis=0, keepdims=True)
        weights = (shifted * (1.0 / total)).astype(BF16)
        log_ref[0, head : head + 1, :] = top + jnp.log(total)
        values = jnp.transpose(v_ref[:, lanes].astype(F32)).astype(BF16)
        mixed = dims(values, weights, 1, 0)
        mixed_ref[:, lanes] = jnp.transpose(mixed).astype(BF16)


def attend_backward(
    padded_half, rows, place_ref, note_ref, q_ref, k_ref, v_ref, g_ref, log_ref, out_ref, sum_ref
):
    visible = key_visible(note_ref, padded_half, rows)
    for head in range(2):
        lanes = slice(head * HD, (head + 1) * HD)
        queries, keys = q_ref[:, lanes] * (HD ** -0.5), k_ref[:, lanes] * (HD ** -0.5)
        values, grads = v_ref[:, lanes], g_ref[:, lanes]
        scores = dims(k_ref[:, lanes], queries, 1, 1)
        weights = jnp.where(visible, jnp.exp(scores - log_ref[0, head : head + 1, :]), 0.0)
        grad_weights = dims(values, grads, 1, 1)
        inner = jnp.sum(weights * grad_weights, axis=0, keepdims=True)
        grad_scores = (weights * (grad_weights - inner)).astype(BF16)
        keys_t = jnp.transpose(keys.astype(F32)).astype(BF16)
        grad_q = jnp.transpose(dims(keys_t, grad_scores, 1, 0)).astype(BF16)
        grad_v = dims(weights.astype(BF16), grads, 1, 0).astype(BF16)
        out_ref[0, :, lanes] = grad_q
        out_ref[1, :, lanes] = dims(grad_scores, queries, 1, 0).astype(BF16)
        out_ref[2, :, lanes] = grad_v
        sum_ref[0, 0:1, lanes] = jnp.sum(grad_q.astype(F32), axis=0, keepdims=True)
        sum_ref[0, 1:2, lanes] = jnp.sum(grad_v.astype(F32), axis=0, keepdims=True)


def attention(place, image, qkv, rows):
    tokens, width = qkv.shape
    pairs = width // 3 // (2 * HD)
    part = lambda p: pl.BlockSpec((tokens, 2 * HD), lambda j, n, p=p: (0, p * pairs + j))
    return run(
        functools.partial(attend_forward, tokens // 2, rows),
        "attention",
        (pairs,),
        place,
        (image, qkv, qkv, qkv),
        [pl.BlockSpec((16, 128), lambda j, n: (rows // 16, 0)), part(0), part(1), part(2)],
        [
            ((tokens, width // 3), BF16, pl.BlockSpec((tokens, 2 * HD), lambda j, n: (0, j))),
            ((pairs, 2, tokens), F32, pl.BlockSpec((1, 2, tokens), lambda j, n: (j, 0, 0))),
        ],
    )


def attention_grad(place, image, qkv, grad_mixed, log_total, rows):
    tokens, width = qkv.shape
    pairs = width // 3 // (2 * HD)
    part = lambda p: pl.BlockSpec((tokens, 2 * HD), lambda j, n, p=p: (0, p * pairs + j))
    return run(
        functools.partial(attend_backward, tokens // 2, rows),
        "attention_grad",
        (pairs,),
        place,
        (image, qkv, qkv, qkv, grad_mixed, log_total),
        [
            pl.BlockSpec((16, 128), lambda j, n: (rows // 16, 0)),
            part(0),
            part(1),
            part(2),
            pl.BlockSpec((tokens, 2 * HD), lambda j, n: (0, j)),
            pl.BlockSpec((1, 2, tokens), lambda j, n: (j, 0, 0)),
        ],
        [
            (
                (3, tokens, width // 3),
                BF16,
                pl.BlockSpec((3, tokens, 2 * HD), lambda j, n: (0, 0, j)),
            ),
            ((pairs, 8, 2 * HD), F32, pl.BlockSpec((1, 8, 2 * HD), lambda j, n: (j, 0, 0))),
        ],
    )


def norm_one_body(place_ref, own_ref, other_ref, gain_ref, shift_ref, image_ref, low_ref):
    def write(values_ref):
        normal, _ = normalize(values_ref[...].astype(F32))
        image_ref[...] = values_ref[...]
        low_ref[...] = (normal * gain_ref[...] + shift_ref[...]).astype(BF16)

    mine = pl.program_id(0) == place_ref[0]
    pl.when(mine)(lambda: write(own_ref))
    pl.when(jnp.logical_not(mine))(lambda: write(other_ref))


def norm_one(place, own, other, gain, shift):
    padded, width = own.shape
    rows = pl.BlockSpec((padded, width), lambda i, n: (i, 0))
    shape = (2 * padded, width)
    return run(
        norm_one_body,
        "norm_one",
        (2,),
        place,
        (own, other, gain, shift),
        [whole(padded, width)] * 2 + [whole(1, width)] * 2,
        [(shape, BF16, rows)] * 2,
    )


def norm_two_body(
    place_ref, image_ref, own_ref, other_ref, bias_ref, gain_ref, shift_ref, middle_ref, low_ref
):
    branch = own_ref[...].astype(F32) + other_ref[...].astype(F32)
    middle = image_ref[...].astype(F32) + branch + bias_ref[...]
    normal, _ = normalize(middle)
    middle_ref[...] = middle
    low_ref[...] = (normal * gain_ref[...] + shift_ref[...]).astype(BF16)


def norm_two(place, image, own, other, bias, gain, shift):
    tokens, width = image.shape
    rows = pl.BlockSpec((tokens // 2, width), lambda i, n: (i, 0))
    return run(
        norm_two_body,
        "norm_two",
        (2,),
        place,
        (image, own, other, bias, gain, shift),
        [rows] * 3 + [whole(1, width)] * 3,
        [((tokens, width), F32, rows), ((tokens, width), BF16, rows)],
    )


def add_sums(sum_ref, values):
    @pl.when(pl.program_id(0) == 0)
    def _():
        sum_ref[...] = jnp.zeros_like(sum_ref)

    for k, value in enumerate(values):
        sum_ref[k : k + 1, :] += jnp.sum(value, axis=0, keepdims=True)


def norm_two_back_body(
    place_ref, incoming_ref, own_ref, other_ref, middle_ref, gain_ref, grad_ref, low_ref, sum_ref
):
    incoming = incoming_ref[...].astype(F32)
    grad = own_ref[...].astype(F32) + other_ref[...].astype(F32)
    normal, scale = normalize(middle_ref[...])
    grad_middle = incoming + normalize_grad(grad, gain_ref[...], normal, scale)
    low = grad_middle.astype(BF16)
    grad_ref[...] = grad_middle
    low_ref[...] = low
    add_sums(sum_ref, (grad * normal, grad, low.astype(F32), incoming))


def norm_two_back(place, incoming, own, other, middle, gain):
    tokens, width = incoming.shape
    rows = pl.BlockSpec((tokens // 2, width), lambda i, n: (i, 0))
    return run(
        norm_two_back_body,
        "norm_two_back",
        (2,),
        place,
        (incoming, own, other, middle, gain),
        [rows] * 4 + [whole(1, width)],
        [((tokens, width), F32, rows), ((tokens, width), BF16, rows), ((8, width), F32, whole(8, width))],
    )


def norm_one_back_body(
    place_ref, grad_ref, own_ref, other_ref, image_ref, gain_ref, kept_ref, low_ref, sum_ref
):
    grad = own_ref[...].astype(F32) + other_ref[...].astype(F32)
    normal, scale = normalize(image_ref[...].astype(F32))
    total = grad_ref[...] + normalize_grad(grad, gain_ref[...], normal, scale)
    add_sums(sum_ref, (grad * normal, grad))

    @pl.when(pl.program_id(0) == place_ref[0])
    def _():
        kept_ref[...] = total
        low_ref[...] = total.astype(BF16)


def norm_one_back(place, grad_middle, own, other, image, gain):
    tokens, width = image.shape
    padded = tokens // 2
    rows = pl.BlockSpec((padded, width), lambda i, n: (i, 0))
    return run(
        norm_one_back_body,
        "norm_one_back",
        (2,),
        place,
        (grad_middle, own, other, image, gain),
        [rows] * 4 + [whole(1, width)],
        [
            ((padded, width), F32, whole(padded, width)),
            ((padded, width), BF16, whole(padded, width)),
            ((8, width), F32, whole(8, width)),
        ],
    )


def split_body(part_rows, place_ref, keep_in, send_in, keep, send, *parts):
    keep[...] = keep_in[...]
    send[...] = send_in[...]
    if parts:
        first = pl.multiple_of(place_ref[1] * part_rows, part_rows)
        parts[0][...] = keep_in[pl.ds(first, part_rows), :]
        parts[1][...] = send_in[pl.ds(first, part_rows), :]


def split_columns(place, shard, number, part_rows, name):
    depth, wide = shard.shape
    one = wide // number // 2
    out = lambda rows: ((rows, wide // 2), BF16, pl.BlockSpec((rows, one), lambda j, n: (0, j)))
    return run(
        functools.partial(split_body, part_rows),
        name,
        (number,),
        place,
        (shard, shard),
        [
            pl.BlockSpec((depth, one), lambda j, n: (0, 2 * j + n[0])),
            pl.BlockSpec((depth, one), lambda j, n: (0, 2 * j + 1 - n[0])),
        ],
        [out(depth)] * 2 + ([out(part_rows)] * 2 if part_rows else []),
    )


def pair_body(rows, place_ref, own_ref, other_ref, out_ref):
    first = pl.multiple_of(place_ref[1] * rows, rows)
    zero = place_ref[0] == 0
    own, other = own_ref[pl.ds(first, rows), :], other_ref[pl.ds(first, rows), :]
    out_ref[:rows, :] = jnp.where(zero, own, other)
    out_ref[rows:, :] = jnp.where(zero, other, own)


def pair_part(place, own, other, rows):
    depth, wide = own.shape
    tile = wide // 2
    return run(
        functools.partial(pair_body, rows),
        "pair_part",
        (2,),
        place,
        (own, other),
        [pl.BlockSpec((depth, tile), lambda j, n: (0, j))] * 2,
        [((2 * rows, wide), BF16, pl.BlockSpec((2 * rows, tile), lambda j, n: (0, j)))],
    )[0]


def join_body(blocks, count, finish, place_ref, left_ref, bias_ref, *refs):
    pieces, joined_ref, outs = refs[:count], refs[count], refs[count + 1 :]
    for k, (number, source, rows) in enumerate(blocks):
        first = pl.multiple_of(place_ref[k] * rows, rows)
        joined_ref[pl.ds(first, rows), :] = pieces[number][source : source + rows, :]
    total = dims(left_ref[...], joined_ref[...], 1, 0) + bias_ref[...]
    for out, value in zip(outs, finish(total)):
        out[...] = value.astype(out.dtype)


def join_dot(line, left, pieces, bias, finish, results, tile, name):
    arrays = []
    for piece in pieces:
        if not any(piece[0] is array for array in arrays):
            arrays.append(piece[0])
    number = lambda array: [array is other for other in arrays].index(True)
    blocks = [(number(array), source, rows) for array, source, rows, _ in pieces]
    place = line.gate(numbers(*[piece[3] for piece in pieces]))
    tokens, depth = left.shape
    wide = arrays[0].shape[1]
    spec = lambda rows: pl.BlockSpec((rows, tile), lambda j, n: (0, j))
    return line.mark(
        run(
            functools.partial(join_body, blocks, len(arrays), finish),
            name,
            (wide // tile,),
            place,
            (left, bias) + tuple(arrays),
            [whole(tokens, depth), spec(1)] + [spec(array.shape[0]) for array in arrays],
            [((depth, wide), BF16, spec(depth))] + [((tokens, wide), BF16, spec(tokens))] * results,
        )
    )


def activate(hidden):
    normal = 0.5 * (1.0 + lax.erf(hidden * math.sqrt(0.5)))
    density = jnp.exp(-0.5 * hidden * hidden) * (1.0 / math.sqrt(2.0 * math.pi))
    return hidden * normal, normal + hidden * density


def feed_back_body(
    own_blocks, count, place_ref, incoming_ref, act_ref, slope_ref, own_ref, *refs
):
    others, (low_ref, sum_ref, part_ref), (weight_ref, total_ref) = (
        refs[:count],
        refs[count : count + 3],
        refs[count + 3 :],
    )
    step = pl.program_id(0)

    @pl.when(step < own_blocks)
    def _():
        weight_ref[...] = own_ref[...]

    for k in range(count):

        @pl.when(step == own_blocks + k)
        def _(k=k):
            weight_ref[...] = others[k][...]

    grad = dims(incoming_ref[...], weight_ref[...], 1, 1) * slope_ref[...].astype(F32)
    low = grad.astype(BF16)
    low_ref[...] = low
    sum_ref[...] = jnp.sum(low.astype(F32), axis=0, keepdims=True)
    part = dims(act_ref[...], weight_ref[...], 1, 0)
    total = jnp.where(step == 0, part, total_ref[...] + part)
    total_ref[...] = total

    @pl.when(step == own_blocks + count - 1)
    def _():
        part_ref[...] = total.astype(BF16)


def feed_back(place, incoming, act, slope, own, others):
    tokens, width = incoming.shape
    hidden = act.shape[1]
    tile = others[0].shape[0]
    own_blocks = own.shape[0] // tile
    steps = own_blocks + len(others)
    block = pl.BlockSpec((tokens, tile), lambda s, n: (0, n[s]))
    return run(
        functools.partial(feed_back_body, own_blocks, len(others)),
        "feed_back",
        (steps,),
        place,
        (incoming, act, slope, own) + tuple(others),
        [
            whole(tokens, width),
            block,
            block,
            pl.BlockSpec((tile, width), lambda s, n: (jnp.minimum(s, own_blocks - 1), 0)),
        ]
        + [whole(tile, width)] * len(others),
        [
            ((tokens, hidden), BF16, block),
            ((1, hidden), F32, pl.BlockSpec((1, tile), lambda s, n: (0, n[s]))),
            ((tokens, width), BF16, whole(tokens, width)),
        ],
        [pltpu.VMEM((tile, width), BF16), pltpu.VMEM((tokens, width), F32)],
    )


def dot_rows_body(place_ref, left_ref, weight_ref, out_ref):
    parts = left_ref.shape[0] if len(left_ref.shape) == 3 else 1
    if parts == 1:
        total = dims(left_ref[...], weight_ref[...], 1, 1)
    else:
        one = left_ref.shape[2]
        total = dims(left_ref[0], weight_ref[:, :one], 1, 1)
        for p in range(1, parts):
            total = total + dims(left_ref[p], weight_ref[:, p * one : (p + 1) * one], 1, 1)
    out_ref[...] = total.astype(BF16)


def dot_rows(place, left, weight, tile, name):
    tokens = left.shape[-2]
    rows, depth = weight.shape
    return run(
        dot_rows_body,
        name,
        (rows // tile,),
        place,
        (left, weight),
        [whole(*left.shape), pl.BlockSpec((tile, depth), lambda j, n: (j, 0))],
        [((tokens, rows), BF16, pl.BlockSpec((tokens, tile), lambda j, n: (0, j)))],
    )[0]


def pack_body(columns, owned, replicas, share, place_ref, two_ref, one_ref, qv_ref, up_ref, out_ref):
    zero = place_ref[0] == 0
    pairs = qv_ref.shape[0] // columns
    hidden = up_ref.shape[1] // columns
    out_ref[...] = jnp.zeros_like(out_ref)
    for x in range(columns):
        parts = [qv_ref[x * pairs + p, row : row + 1, :] for row in range(2) for p in range(pairs)]
        for ref, row in ((two_ref, 2), (one_ref, 0), (one_ref, 1), (two_ref, 0), (two_ref, 1), (two_ref, 3)):
            first, second = (
                ref[row : row + 1, (2 * x + c) * owned : (2 * x + c + 1) * owned] for c in range(2)
            )
            parts.append(jnp.where(zero, first, second))
        parts.append(up_ref[:, x * hidden : (x + 1) * hidden])
        row = jnp.concatenate(parts, axis=1)
        for p in range(out_ref.shape[1] // 8):
            out_ref[x, 8 * p : 8 * p + 1, :share] = row[:, p * share : (p + 1) * share]


def out_grad_body(count, replicas, place_ref, left_ref, right_ref, vec_ref, *rest):
    total = dims(left_ref[...], right_ref[...], 0, 0)
    height = total.shape[0] // replicas
    every = height + 8
    for z in range(replicas):
        for first, value in (
            (z * every, total[z * height : (z + 1) * height]),
            (z * every + height, vec_ref[0, 8 * z : 8 * z + 8, :]),
        ):
            rows = slice(first, first + value.shape[0])
            for added in rest[:count]:
                value = value + added[rows, :].astype(F32)
            rest[count][rows, :] = value.astype(BF16)


def out_grad(place, left, right, vectors, height, replicas, added=()):
    tokens, width = right.shape
    every = height + 8 * replicas
    if height % 128:
        left = lax.dynamic_slice_in_dim(left, place[0] * height, height, 1)
        place = place * numbers(0, 1, 1)
    return run(
        functools.partial(out_grad_body, len(added), replicas),
        "out_grad",
        (1,),
        place,
        (left, right, vectors) + tuple(added),
        [
            pl.BlockSpec((tokens, height), lambda i, n: (0, n[0])),
            whole(tokens, width),
            pl.BlockSpec((1, 8 * replicas, width), lambda i, n: (n[1], n[2], 0)),
        ]
        + [whole(every, width)] * len(added),
        [((every, width), BF16, whole(every, width))],
    )[0]


def weight_grad_body(count, index_ref, left_ref, right_ref, *rest):
    total = dims(left_ref[...], right_ref[...], 0, 0)
    for added in rest[:count]:
        total = total + added[...].astype(F32)
    rest[count][...] = total.astype(BF16)


def weight_grad(left, right, blocks, height, added=()):
    tokens = left.shape[0]
    number = blocks.shape[0]
    if height % 128:
        narrow = [
            lax.dynamic_slice_in_dim(left, blocks[i] * height, height, 1) for i in range(number)
        ]
        left = jnp.concatenate(narrow, axis=1)
        blocks = jnp.zeros((1,), jnp.int32)
        number, height = 1, number * height
    parts = right.shape[0] if right.ndim == 3 else 1
    width = right.shape[-1]
    if right.ndim == 3:
        right_spec = pl.BlockSpec((pl.Squeezed(), tokens, width), lambda j, i, n: (j, 0, 0))
    else:
        parts = 2
        width = width // parts
        right_spec = pl.BlockSpec((tokens, width), lambda j, i, n: (0, j))
    tile = pl.BlockSpec((height, width), lambda j, i, n: (i, j))
    return pl.pallas_call(
        functools.partial(weight_grad_body, len(added)),
        grid_spec=pltpu.PrefetchScalarGridSpec(
            num_scalar_prefetch=1,
            grid=(parts, number),
            in_specs=[pl.BlockSpec((tokens, height), lambda j, i, n: (0, n[i])), right_spec]
            + [tile] * len(added),
            out_specs=tile,
        ),
        out_shape=jax.ShapeDtypeStruct((number * height, parts * width), BF16),
        compiler_params=pltpu.CompilerParams(vmem_limit_bytes=VMEM_LIMIT),
        cost_estimate=HINT,
        name="weight_grad",
    )(blocks, left, right, *added)


def tick_body(place_ref, out_ref):
    out_ref[...] = jnp.full(out_ref.shape, place_ref[0], jnp.int32)


class Line:
    def __init__(self):
        self.last = None

    def gate(self, value):
        if self.last is None:
            return value
        return lax.optimization_barrier((value, self.last))[0]

    def mark(self, value):
        self.last = value
        return value

    def tick(self):
        place = self.gate(jnp.zeros((1,), jnp.int32))
        self.last = run(
            tick_body, "tick", (1,), place, (), [], [((8, 128), jnp.int32, whole(8, 128))]
        )[0]

    def pass_on(self, value):
        self.tick()
        return self.mark(self.gate(value))


def normalize(values):
    centered = values - jnp.mean(values, -1, keepdims=True)
    scale = lax.rsqrt(jnp.mean(centered * centered, -1, keepdims=True) + EPS)
    return centered * scale, scale


def normalize_grad(grad, gain, normal, scale):
    scaled = grad * gain
    return scale * (
        scaled
        - jnp.mean(scaled, -1, keepdims=True)
        - normal * jnp.mean(scaled * normal, -1, keepdims=True)
    )


def place(buffer, piece, position):
    start = (position,) + (0,) * (buffer.ndim - 1)
    return lax.dynamic_update_slice(buffer, piece[None], start)


def pick(array, index, axis=0):
    return lax.dynamic_index_in_dim(array, index, axis, keepdims=False)


def shards(
    tokens,
    lengths,
    qkv_weight,
    query_bias,
    value_bias,
    out_weight,
    out_bias,
    first_gain,
    first_shift,
    second_gain,
    second_shift,
    up_weight,
    up_bias,
    down_weight,
    down_bias,
    cotangent,
):
    _, rows, width = tokens.shape
    halves = lax.axis_size("seq")
    group = lax.axis_size("shard")
    replicas = lax.axis_size("rep")
    columns = group // 2
    half, member, copy_id = (lax.axis_index(name) for name in ("seq", "shard", "rep"))
    core, column = member % 2, member // 2
    owned = width // group
    owned_hidden = up_bias.shape[0]
    padded = -(-(rows + 1) // 16) * 16

    def over_core(value):
        return lax.ppermute(value, "shard", [(i, i ^ 1) for i in range(group)])

    def over_x(value, step):
        return lax.ppermute(value, "shard", [(i, (i + 2 * step) % group) for i in range(group)])

    def over_x_core(value, step):
        pairs = [(i, ((i + 2 * step) % group) ^ 1) for i in range(group)]
        return lax.ppermute(value, "shard", pairs)

    def over_y(value):
        return lax.ppermute(value, "seq", [(i, halves - 1 - i) for i in range(halves)])

    def over_z(value, step):
        return lax.ppermute(value, "rep", [(i, i ^ step) for i in range(replicas)])

    swaps = []
    for s in range(halves):
        for h in range(group):
            if s != h % 2:
                swaps.append((s * group + h, (h % 2) * group + (h // 2) * 2 + s))

    def swap(value):
        return lax.ppermute(value, ("seq", "shard"), swaps)

    def by_core(mine, other, axis=0):
        return jnp.where(
            core == 0, jnp.stack([mine, other], axis), jnp.stack([other, mine], axis)
        )

    line = Line()
    steps = range(1, columns)
    other_half = halves - 1 - half
    side = copy_id % 2
    quarter = half * 2 + side

    length = lengths[0]
    lane = lax.broadcasted_iota(jnp.int32, (padded - rows, width), 1)
    note = jnp.where(lane == 0, length // 16, jnp.where(lane == 1, length % 16, 0)).astype(BF16)
    own_half = lambda shard: pick(
        shard.reshape(halves, shard.shape[0] // halves, shard.shape[1]), half
    )
    source = lambda k: (column - k) % columns
    part = owned // halves
    eighth = owned // halves // 2
    chunks = 2

    def relay_qkv(index, c):
        for k in steps:
            value = line.pass_on(qkv_x[index][k - 1])
            at = (2 * source(k) + c) * halves
            qkv_pieces.append((value, 0, part, at + half))
            qkv_pieces.append((over_y(value), 0, part, at + other_half))

    qkv_x = {}

    own_tokens = line.mark(jnp.concatenate([line.gate(tokens[0]), note], axis=0))
    other_tokens = swap(own_tokens)
    singles = [
        query_bias,
        value_bias,
        out_bias,
        first_gain,
        first_shift,
        second_gain,
        second_shift,
        down_bias,
    ]
    singles += [up_bias[i * owned : (i + 1) * owned] for i in range(owned_hidden // owned)]
    row_of = lax.broadcasted_iota(jnp.int32, (16, owned), 0)
    vectors = jnp.zeros((16, owned), BF16)
    for i, single in enumerate(singles):
        vectors = jnp.where(row_of == i, jnp.broadcast_to(single[None], (16, owned)), vectors)
    vectors = line.mark(line.gate(vectors))
    vec_x = [over_x(vectors, k) for k in steps]
    qkv_keep, qkv_send, qkv_part, qkv_cross = line.mark(
        split_columns(
            line.gate(numbers(core, half)), qkv_weight, 3 * columns, owned // halves, "split_qkv"
        )
    )
    qkv_x[0] = [over_x(qkv_part, k) for k in steps]
    qkv_x[1] = [over_x_core(line.gate(qkv_cross), k) for k in steps]
    qkv_core = over_core(line.gate(qkv_send))
    qkv_core = line.pass_on(qkv_core)
    qkv_pieces = [
        (qkv_keep, 0, owned, member),
        (qkv_core, 0, owned, member + 1 - 2 * core),
    ]
    relay_qkv(0, core)
    own_image = line.mark(jnp.where(half == core, own_tokens, line.pass_on(other_tokens)))
    other_image = over_core(own_image)
    other_image = line.pass_on(other_image)
    up_keep, up_send = line.mark(
        split_columns(line.gate(numbers(core, half)), up_weight, columns, 0, "split_up")
    )
    gathered_vec = jnp.zeros((columns,) + vectors.shape, BF16)
    gathered_vec = place(gathered_vec, vectors, column)
    for k in steps:
        gathered_vec = place(gathered_vec, line.pass_on(vec_x[k - 1]), (column - k) % columns)
    line.mark(gathered_vec)
    vec_core = over_core(gathered_vec)
    up_core = over_core(line.gate(up_send))
    up_core = line.pass_on(up_core)
    up_part = line.mark(pair_part(line.gate(numbers(core, quarter)), up_keep, up_core, eighth))
    out_part = line.mark(own_half(line.gate(out_weight)))
    out_x = [over_x(line.gate(out_part), k) for k in steps]
    vec_core = line.pass_on(vec_core)
    mine_vec = gathered_vec.astype(F32)
    all_vec = by_core(gathered_vec, vec_core, 1).reshape(columns * 2, 16, owned)
    all_vec = all_vec.astype(F32)
    vec = lambda i: all_vec[:, i].reshape(1, width)
    own_vec = lambda i: mine_vec[:, i].reshape(1, width // 2)
    gain_one, shift_one, gain_two, shift_two = vec(3), vec(4), vec(5), vec(6)
    vec_out, vec_down = vec(2), vec(7)
    vec_up = mine_vec[:, 8 : 8 + owned_hidden // owned].reshape(1, columns * owned_hidden)
    vec_qkv = jnp.concatenate(
        [own_vec(0), jnp.zeros((1, width // 2), F32), own_vec(1)], axis=1
    )
    up_x = [over_x(line.gate(up_part), k) for k in steps]
    image, first_low = line.mark(
        norm_one(line.gate(numbers(core)), own_image, other_image, gain_one, shift_one)
    )
    own_cotangent = line.mark(
        jnp.concatenate([line.gate(cotangent[0]), jnp.zeros((padded - rows, width), BF16)], axis=0)
    )
    down_part = line.mark(own_half(line.gate(down_weight)).reshape(chunks, -1, width))
    relay_qkv(1, 1 - core)
    out_pieces = [(out_weight, 0, owned, column)]
    for k in steps:
        value = line.pass_on(out_x[k - 1])
        at = source(k) * halves
        out_pieces += [(value, 0, part, at + half), (over_y(value), 0, part, at + other_half)]
    down_x = [[over_x(line.gate(down_part[0]), k) for k in steps]]
    wqkv, qkv = join_dot(
        line, first_low, qkv_pieces, vec_qkv, lambda total: (total,), 1, width // 2, "project"
    )

    up_pieces = [(up_keep, 0, owned, member), (up_core, 0, owned, member + 1 - 2 * core)]

    def up_rows(value, k, h, s):
        for c in range(2):
            at = (2 * source(k) + c) * halves * 2 + h * 2 + s
            up_pieces.append((value, c * eighth, eighth, at))

    up_y, up_z, down_others = [], [], []
    no_bias = jnp.zeros((1, width), F32)

    def relay_down(c):
        for k in steps:
            value = line.pass_on(down_x[c][k - 1])
            at = source(k) * halves * chunks + c
            down_others.append((value, at + half * chunks))
            down_others.append((over_y(value), at + other_half * chunks))

    for k in steps:
        value = line.pass_on(up_x[k - 1])
        up_rows(value, k, half, side)
        up_z.append(over_z(value, 1))
        up_y.append(over_y(value))
    mixed, log_total = line.mark(attention(line.gate(numbers(core)), image, qkv, rows))
    wout, branch = join_dot(
        line, mixed, out_pieces, no_bias, lambda total: (total,), 1, width // 2, "project_out"
    )
    branch_other = over_core(branch)
    other_cotangent = swap(line.gate(own_cotangent))
    for k in steps:
        value = line.pass_on(up_y[k - 1])
        up_rows(value, k, other_half, side)
        up_y[k - 1] = over_z(value, 1)
    relay_down(0)
    for k in steps:
        up_rows(line.pass_on(up_z[k - 1]), k, half, 1 - side)
    line.tick()
    down_x.append([over_x(line.gate(down_part[1]), k) for k in steps])
    middle, second_low = line.mark(
        norm_two(
            line.gate(numbers(core)), image, branch, branch_other, vec_out, gain_two, shift_two
        )
    )
    other_cotangent = line.pass_on(other_cotangent)
    own_incoming = line.mark(jnp.where(half == core, own_cotangent, other_cotangent))
    incoming_other = over_core(own_incoming)
    incoming_other = line.pass_on(incoming_other)
    incoming = line.mark(by_core(own_incoming, incoming_other).reshape(2 * padded, width))
    for k in steps:
        up_rows(line.pass_on(up_y[k - 1]), k, other_half, 1 - side)
    wup, act_low, slope = join_dot(line, second_low, up_pieces, vec_up, activate, 2, 512, "hidden")

    class Total:
        def __init__(self, quadrant, lead, cross, split=False):
            self.quadrant, self.lead, self.cross, self.split = quadrant, lead, cross, split
            self.crossed = not cross
            self.halving, self.done, self.step = True, False, 1

        def along_x(self, y):
            return [self.quadrant((column + k) % columns, y, ()) for k in steps]

        def make_first(self):
            self.sent = self.along_x(other_half)

        def make_second(self):
            self.sent_b = self.along_x(half)

        def first(self):
            self.got = tuple(over_x(line.gate(v), k) for k, v in zip(steps, self.sent))

        def second(self):
            self.got_b = tuple(over_x(line.gate(v), k) for k, v in zip(steps, self.sent_b))

        def third(self):
            line.tick()
            self.from_y = over_y(self.quadrant(column, other_half, self.got))

        def fourth(self):
            line.tick()
            total = self.quadrant(column, half, self.got_b + (self.from_y,))
            height = total.shape[0] // self.lead // replicas
            self.total = total.reshape(self.lead, replicas, height, total.shape[1])
            self.halve()

        def bit(self):
            return (copy_id // self.step) % 2

        def halve(self):
            shape = self.total.shape
            pairs = self.total.reshape((self.lead, shape[1] // 2, 2) + shape[2:])
            self.own = pick(pairs, self.bit(), 2)
            self.from_z = over_z(line.mark(pick(pairs, 1 - self.bit(), 2)), self.step)

        def double(self):
            self.step //= 2
            self.from_z = over_z(self.total, self.step)
            if self.split and self.step == 1:
                self.early = over_y(self.total)

        def joined(self, own, got):
            return jnp.where(
                self.bit() == 0, jnp.stack([own, got], 1), jnp.stack([got, own], 1)
            ).reshape((-1,) + own.shape[1:])

        def turn(self):
            line.tick()
            if self.halving:
                own = line.gate(self.own).astype(F32)
                self.total = line.mark((own + self.from_z.astype(F32)).astype(BF16))
                self.step *= 2
                if self.step < replicas:
                    self.halve()
                    return
                self.halving = False
                total = self.total.reshape((self.lead,) + self.total.shape[2:])
                if self.cross:
                    self.own = pick(total, core)
                    self.from_core = over_core(line.mark(pick(total, 1 - core)))
                    return
                self.total = total
                self.double()
            elif not self.crossed:
                self.crossed = True
                own, got = line.gate(self.own), self.from_core
                self.total = line.mark(self.cross(own, got))[None]
                self.double()
            elif self.step:
                if self.split and self.step == 1:
                    self.from_z = line.mark(line.gate(self.from_z))
                    late = over_y(self.from_z)
                    self.total = self.joined(self.total, self.from_z)
                    self.from_y = self.joined(self.early, late)
                    self.step = 0
                    return
                self.total = line.mark(self.joined(line.gate(self.total), self.from_z))
                if self.step > 1:
                    self.double()
                else:
                    self.step = 0
                    self.from_y = over_y(self.total)

        def finish(self):
            while self.step:
                self.turn()
            line.tick()
            total, got = line.gate(self.total), self.from_y
            return line.mark(
                jnp.where(half == 0, jnp.stack([total, got], 0), jnp.stack([got, total], 0)).astype(
                    F32
                )
            )

    def cross_cores(blocks):
        def exchange(own, got):
            one = own.shape[1] // blocks
            left = jnp.where(core == 0, own, got)
            right = jnp.where(core == 0, got, own)
            cols = []
            for k in range(blocks):
                cols += [left[:, k * one : (k + 1) * one], right[:, k * one : (k + 1) * one]]
            return jnp.concatenate(cols, axis=1)

        return exchange

    def by_row(left, right):
        height = owned // halves

        def quadrant(x, y, added):
            blocks = numbers(*[(x * 2 + i) * halves + y for i in range(2)])
            return line.mark(weight_grad(left, right, line.gate(blocks), height, added))

        return quadrant

    def down_quadrant(x, y, added):
        blocks = line.gate(numbers(x * halves + y))
        return line.mark(weight_grad(act_low, incoming, blocks, owned_hidden // halves, added))

    def out_quadrant(x, y, added):
        at = line.gate(numbers(x * halves + y, x, y))
        return line.mark(
            out_grad(at, mixed, branch_low, vec_grads, owned // halves, replicas, added)
        )

    pieces = halves * replicas
    total_down = Total(down_quadrant, 1, None)
    total_down.make_first()
    total_down.first()
    total_down.make_second()
    relay_down(1)
    blocks = halves * chunks
    at = [column * blocks + h for h in range(blocks)] + [place_ for _, place_ in down_others]
    hidden_low, up_sums, partial = line.mark(
        feed_back(
            line.gate(numbers(*at)),
            incoming,
            act_low,
            slope,
            down_weight,
            [value for value, _ in down_others],
        )
    )
    total_down.second()
    grad_second = line.mark(
        dot_rows(line.gate(numbers(core)), hidden_low, wup, width // 2, "grad_second")
    )
    grad_second_other = over_core(grad_second)
    total_up = Total(by_row(second_low, hidden_low), 2, cross_cores(columns), True)
    total_up.make_first()
    total_down.third()
    total_up.first()
    grad_middle, branch_low, sums_two = line.mark(
        norm_two_back(
            line.gate(numbers(core)), incoming, grad_second, grad_second_other, middle, gain_two
        )
    )
    grad_mixed = line.mark(
        dot_rows(line.gate(numbers(core)), branch_low, wout, width // 2, "grad_mixed")
    )
    grad_qkv, qv_sums = line.mark(
        attention_grad(line.gate(numbers(core)), image, qkv, grad_mixed, log_total, rows)
    )
    grad_first = line.mark(
        dot_rows(line.gate(numbers(core)), grad_qkv, wqkv, width // 2, "grad_first")
    )
    grad_first_other = over_core(grad_first)
    total_qkv = Total(by_row(first_low, grad_qkv), 2, cross_cores(3 * columns), True)
    total_qkv.make_first()
    total_down.fourth()
    total_up.make_second()
    total_up.second()
    own_grad, own_grad_low, sums_one = line.mark(
        norm_one_back(
            line.gate(numbers(core)), grad_middle, grad_first, grad_first_other, image, gain_one
        )
    )
    entries = 8 * owned + owned_hidden
    vec_grads = line.mark(
        run(
            functools.partial(pack_body, columns, owned, replicas, entries // pieces),
            "pack_vectors",
            (1,),
            line.gate(numbers(core)),
            (sums_two, sums_one, qv_sums, up_sums),
            [
                whole(8, width),
                whole(8, width),
                whole(*qv_sums.shape),
                whole(*up_sums.shape),
            ],
            [((columns, 8 * pieces, width), F32, whole(columns, 8 * pieces, width))],
        )[0]
    )
    total_out = Total(out_quadrant, 1, None)
    total_out.make_first()
    total_qkv.make_second()
    total_out.make_second()
    total_down.turn()
    total_qkv.first()
    halves_of = lambda value: value.reshape(2, padded, width)
    from_other = over_core(line.pass_on(pick(halves_of(partial), 1 - core)))
    block = pick(halves_of(middle), core) + pick(halves_of(partial), core).astype(F32)
    block = line.mark((line.gate(block) + from_other.astype(F32) + vec_down).astype(BF16))
    total_down.turn()
    total_qkv.second()
    total_qkv.third()
    total_up.third()
    total_down.turn()
    total_up.fourth()
    total_out.first()
    total_up.turn()
    total_down.turn()
    total_up.turn()
    grad_down = total_down.finish().reshape(owned_hidden, width)
    total_qkv.fourth()
    total_up.turn()
    total_up.turn()
    block_moved = swap(line.gate(block))
    total_out.second()
    total_qkv.turn()
    total_out.third()
    total_out.fourth()
    total_qkv.turn()
    total_qkv.turn()
    total_out.turn()
    total_qkv.turn()
    block_out = line.mark(jnp.where(half == core, line.gate(block), block_moved)[:rows][None])
    total_up.turn()
    moved = swap(line.gate(own_grad_low))
    total_out.turn()
    total_qkv.turn()
    total_out.turn()
    grad_qkv_w = total_qkv.finish().reshape(owned, 3 * width)
    total_out.turn()
    out_rows = total_out.finish()
    height = out_rows.shape[2] - 8
    grad_out = out_rows[:, :, :height].reshape(owned, width)
    token_grad = line.mark(
        jnp.where(half == core, line.gate(own_grad), moved.astype(F32))[:rows][None]
    )
    grad_up = total_up.finish().reshape(owned, up_weight.shape[1])

    vec_out_grads = out_rows[:, :, height, : entries // pieces].reshape(entries)
    vec_of = lambda i: vec_out_grads[i * owned : (i + 1) * owned]
    return (
        block_out,
        token_grad,
        grad_qkv_w,
        vec_of(0),
        vec_of(1),
        grad_out,
        vec_of(2),
        vec_of(3),
        vec_of(4),
        vec_of(5),
        vec_of(6),
        grad_up,
        vec_out_grads[8 * owned :],
        grad_down,
        vec_of(7),
    )


def solution(mesh):
    return jax.shard_map(
        shards,
        mesh=mesh,
        in_specs=(
            P(("shard", "rep"), "seq", None),
            P(("shard", "rep")),
            P("shard", None),
            P("shard"),
            P("shard"),
            P("shard", None),
            P("shard"),
            P("shard"),
            P("shard"),
            P("shard"),
            P("shard"),
            P("shard", None),
            P("shard"),
            P("shard", None),
            P("shard"),
            P(("shard", "rep"), "seq", None),
        ),
        out_specs=(
            P(("shard", "rep"), "seq", None),
            P(("shard", "rep"), "seq", None),
            P("shard", None),
            P("shard"),
            P("shard"),
            P("shard", None),
            P("shard"),
            P("shard"),
            P("shard"),
            P("shard"),
            P("shard"),
            P("shard", None),
            P("shard"),
            P("shard", None),
            P("shard"),
        ),
        check_vma=False,
    )
```
